128 devices in a mesh: gy: 2 (over y_hi), gx: 64 (over x, y_lo, z, core).
Axes of the slice: x: 4, y: 4 (y_hi: 2, y_lo: 2; y = y_hi * 2 + y_lo), z: 4, core: 2. Of those that a mesh axis runs over, the one named last changes fastest.
Arguments:
- radar_frame: bfloat16 [256, 1024, 128], P('gy', 'gx'), may hold values from -6 to 6
- lstm_state: bfloat16 [256, 1024, 128], P('gy', 'gx'), may hold values from -6 to 6
- w_conv: bfloat16 [3, 3, 192, 256], replicated, may hold values from -0.15625 to 0.15625
- b_gates: float32 [256], replicated, may hold values from -6 to 6
- norm_gain: float32 [64], replicated, may hold values from 0.5 to 2
- w_qkv: bfloat16 [64, 384], replicated, may hold values from -1 to 1
- w_out: bfloat16 [128, 64], replicated, may hold values from -1.25 to 1.25
- state_grad: bfloat16 [256, 1024, 128], P('gy', 'gx'), may hold values from -6 to 6
Outputs:
- new_state: bfloat16 [256, 1024, 128], P('gy', 'gx')
- grad_frame: bfloat16 [256, 1024, 128], P('gy', 'gx')
- grad_state: bfloat16 [256, 1024, 128], P('gy', 'gx')
The draws below stay inside these ranges and needn't reach their ends.
All inputs are finite; a program needn't handle non-finite values.
Results may differ from the reference program's by a relative error of at most 0.014.
The reference program's roundings to bfloat16 on the way count: a program that leaves them out, or rounds other values in their place, can miss the bound.
Values may be sent and summed in bfloat16 or wider, within the bound.
No kernel may reach another device: no remote copies, remote signals or barrier semaphores. Data moves between devices by JAX's collectives and lax.ppermute only.
A program may use at most 128 MiB of HBM per device.

```python
import math
import jax
import jax.numpy as jnp
from jax import lax

W = 1024
CIN = 128
HID = 64
HEADS = 8
HEAD_DIM = 16
GATES = 256
QKV = 384
H = 256


def steps_of(stream_key, shape, split, low, top_value):
    gain = 1.0
    for dim, parts in split:
        draws = jax.random.uniform(jax.random.fold_in(jax.random.fold_in(stream_key, 6), dim), (parts,), jnp.float32, low / len(split), top_value / len(split))
        gain = gain * jnp.repeat(jnp.exp(draws), shape[dim] // parts).reshape((-1,) + (1,) * (len(shape) - 1 - dim))
    return gain


def centred(rng, dims, scale, reach, split=(), held_as=jnp.bfloat16):
    entries = jax.random.normal(rng, dims, jnp.float32) * scale
    if len(split) > 0:
        entries = steps_of(rng, dims, split, -0.22, 0.18) * entries
    return jnp.clip(entries, min=-reach, max=reach).astype(held_as)


def setup_inputs(seed: int = 0) -> dict:
    key_list = jax.random.split(jax.random.key(seed), 9)
    radar_frame = centred(key_list[0], (H, W, CIN), 1.0, 6.0, ((0, 2), (1, 64)))
    lstm_state = centred(key_list[1], (H, W, 2 * HID), 1.0, 6.0, ((0, 2), (1, 64)))
    w_conv = centred(key_list[2], (3, 3, CIN + HID, GATES), (9 * (CIN + HID)) ** -0.5, 0.15625)
    b_gates = centred(key_list[3], (GATES,), 1.0, 6.0, (), jnp.float32)
    norm_gain = jnp.clip(jnp.exp(jax.random.uniform(key_list[4], (HID,), jnp.float32, math.log(0.5), math.log(2.0))), 0.5, 2.0)
    w_qkv = centred(key_list[5], (HID, QKV), (HID // 2) ** -0.5, 1.0)
    w_out = centred(key_list[6], (HEADS * HEAD_DIM, HID), 0.2, 1.25)
    state_grad = centred(key_list[7], (H, W, 2 * HID), 1.0, 6.0, ((0, 2), (1, 64)))
    return dict(radar_frame=radar_frame, lstm_state=lstm_state, w_conv=w_conv, b_gates=b_gates, norm_gain=norm_gain, w_qkv=w_qkv, w_out=w_out, state_grad=state_grad)


EPS = 1e-05

def conv_forward(inputs, w_conv):
    rows_all, cols_all, channels = inputs.shape
    padded = jnp.pad(inputs, ((1, 1), (1, 1), (0, 0)))
    total = jnp.zeros((rows_all * cols_all, w_conv.shape[3]), jnp.float32)
    for row_tap in range(3):
        for col_tap in range(3):
            window = padded[row_tap:row_tap + rows_all, col_tap:col_tap + cols_all].reshape(-1, channels)
            total = total + jnp.dot(window, w_conv[row_tap, col_tap], preferred_element_type=jnp.float32)
    return total.reshape(rows_all, cols_all, -1)

def conv_backward(grad_gates, w_conv):
    rows_all, cols_all, gate_dim = grad_gates.shape
    padded = jnp.pad(grad_gates, ((1, 1), (1, 1), (0, 0)))
    total = jnp.zeros((rows_all * cols_all, w_conv.shape[2]), jnp.float32)
    for row_tap in range(3):
        for col_tap in range(3):
            window = padded[2 - row_tap:2 - row_tap + rows_all, 2 - col_tap:2 - col_tap + cols_all].reshape(-1, gate_dim)
            total = total + jnp.dot(window, w_conv[row_tap, col_tap].T, preferred_element_type=jnp.float32)
    return total.reshape(rows_all, cols_all, -1)

def split_heads(tensor):
    length = tensor.shape[0]
    return tensor.reshape(length, HEADS, HEAD_DIM).transpose(1, 0, 2).astype(jnp.float32)

def join_heads(tensor):
    return tensor.transpose(1, 0, 2).reshape(tensor.shape[1], HEADS * HEAD_DIM)

def row_probs(query_heads, key_heads):
    scores = jnp.einsum('hqd,hkd->hqk', query_heads, key_heads) * HEAD_DIM ** (-0.5)
    exp_scores = jnp.exp(scores)
    return exp_scores / lax.optimization_barrier(jnp.sum(exp_scores, axis=-1, keepdims=True))

def row_forward(pieces):
    queries, key_rows, value_rows = pieces
    probs = row_probs(split_heads(queries), split_heads(key_rows))
    probs_low = lax.optimization_barrier(probs.astype(jnp.bfloat16)).astype(jnp.float32)
    attended = jnp.einsum('hqk,hkd->hqd', probs_low, split_heads(value_rows))
    return join_heads(attended).astype(jnp.bfloat16)

def row_backward(pieces):
    queries, key_rows, value_rows, grad_rows = pieces
    query_heads = split_heads(queries)
    key_heads = split_heads(key_rows)
    value_heads = split_heads(value_rows)
    grad_heads = split_heads(grad_rows)
    probs = row_probs(query_heads, key_heads)
    probs_low = lax.optimization_barrier(probs.astype(jnp.bfloat16)).astype(jnp.float32)
    grad_value = jnp.einsum('hqk,hqd->hkd', probs_low, grad_heads)
    grad_prob = jnp.einsum('hqd,hkd->hqk', grad_heads, value_heads)
    inner = lax.optimization_barrier(jnp.sum(probs * grad_prob, axis=-1, keepdims=True))
    grad_score = lax.optimization_barrier((probs * (grad_prob - inner)).astype(jnp.bfloat16)).astype(jnp.float32)
    grad_query = jnp.einsum('hqk,hkd->hqd', grad_score, key_heads) * HEAD_DIM ** (-0.5)
    grad_key = jnp.einsum('hqk,hqd->hkd', grad_score, query_heads) * HEAD_DIM ** (-0.5)
    return jnp.concatenate([join_heads(grad_query), join_heads(grad_key), join_heads(grad_value)], axis=-1).astype(jnp.bfloat16)

def reference(radar_frame, lstm_state, w_conv, b_gates, norm_gain, w_qkv, w_out, state_grad):
    hidden_dim = HID
    attn_dim = HEADS * HEAD_DIM
    h_prev = lstm_state[..., :hidden_dim]
    c_prev = lstm_state[..., hidden_dim:].astype(jnp.float32)
    inputs = jnp.concatenate([radar_frame, h_prev], axis=-1)
    gates = conv_forward(inputs, w_conv) + b_gates
    in_gate = jax.nn.sigmoid(gates[..., :hidden_dim])
    forget = jax.nn.sigmoid(gates[..., hidden_dim:2 * hidden_dim])
    out_gate = jax.nn.sigmoid(gates[..., 2 * hidden_dim:3 * hidden_dim])
    update = jnp.tanh(gates[..., 3 * hidden_dim:])
    c_new = forget * c_prev + in_gate * update
    cell_tanh = jnp.tanh(c_new)
    h_new = out_gate * cell_tanh
    inv_rms = lax.rsqrt(lax.optimization_barrier(jnp.mean(h_new * h_new, axis=-1, keepdims=True)) + EPS)
    normed = (h_new * inv_rms * norm_gain).astype(jnp.bfloat16)
    qkv = jnp.dot(normed.reshape(-1, hidden_dim), w_qkv, preferred_element_type=jnp.float32).astype(jnp.bfloat16)
    qkv = qkv.reshape(H, W, 3 * attn_dim)
    queries = qkv[..., :attn_dim]
    key_rows = qkv[..., attn_dim:2 * attn_dim]
    value_rows = qkv[..., 2 * attn_dim:]
    attended = lax.map(row_forward, (queries, key_rows, value_rows))
    mixed = h_new + jnp.dot(attended.reshape(-1, attn_dim), w_out, preferred_element_type=jnp.float32).reshape(H, W, hidden_dim)
    new_state = jnp.concatenate([mixed, c_new], axis=-1).astype(jnp.bfloat16)
    grad_mixed = state_grad[..., :hidden_dim]
    grad_attended = jnp.dot(grad_mixed.reshape(-1, hidden_dim), w_out.T, preferred_element_type=jnp.float32).astype(jnp.bfloat16)
    grad_attended = grad_attended.reshape(H, W, attn_dim)
    grad_qkv = lax.map(row_backward, (queries, key_rows, value_rows, grad_attended))
    grad_normed = jnp.dot(grad_qkv.reshape(-1, 3 * attn_dim), w_qkv.T, preferred_element_type=jnp.float32).reshape(H, W, hidden_dim)
    scaled = grad_normed * norm_gain
    grad_hidden = grad_mixed.astype(jnp.float32) + inv_rms * scaled - h_new * inv_rms ** 3 * lax.optimization_barrier(jnp.mean(scaled * h_new, axis=-1, keepdims=True))
    grad_cell = state_grad[..., hidden_dim:].astype(jnp.float32) + grad_hidden * out_gate * (1.0 - cell_tanh * cell_tanh)
    grad_gates = jnp.concatenate([grad_cell * update * in_gate * (1.0 - in_gate), grad_cell * c_prev * forget * (1.0 - forget), grad_hidden * cell_tanh * out_gate * (1.0 - out_gate), grad_cell * in_gate * (1.0 - update * update)], axis=-1).astype(jnp.bfloat16)
    grad_inputs = conv_backward(grad_gates, w_conv)
    grad_frame = grad_inputs[..., :CIN].astype(jnp.bfloat16)
    grad_state = jnp.concatenate([grad_inputs[..., CIN:], grad_cell * forget], axis=-1).astype(jnp.bfloat16)
    return (new_state, grad_frame, grad_state)
```

```python
import jax
import jax.numpy as jnp
from jax import lax
from jax.experimental import pallas as pl
from jax.experimental.pallas import tpu as pltpu
from jax.sharding import PartitionSpec as P

HEADS = 8
EPS = 1e-05
LOG2E = 1.4426950408889634
F32 = jnp.float32
BF16 = jnp.bfloat16


def matmul(lhs, rhs, lhs_dim=1, rhs_dim=0):
    return lax.dot_general(
        lhs, rhs, (((lhs_dim,), (rhs_dim,)), ((), ())), preferred_element_type=F32
    )


def call(body, out_shape, scratch=(), vmem=48):
    return pl.pallas_call(
        body,
        out_shape=out_shape,
        scratch_shapes=list(scratch),
        compiler_params=pltpu.CompilerParams(vmem_limit_bytes=vmem << 20),
    )


def low_half(shape):
    return lax.broadcasted_iota(jnp.int32, shape, 1) < shape[1] // 2


def swap_halves(value):
    return pltpu.roll(value, value.shape[1] // 2, axis=1)


def column_of(shape, cols):
    return lax.rem(lax.broadcasted_iota(jnp.int32, shape, 0), cols)


def spread(edge, cols, at):
    rows = edge.shape[0]
    shape = (rows * cols, rows)
    position = lax.broadcasted_iota(jnp.int32, shape, 0)
    row = lax.broadcasted_iota(jnp.int32, shape, 1)
    pick = jnp.where(position == row * cols + at, 1.0, 0.0).astype(BF16)
    return matmul(pick, edge)


def pick_column(flat, cols, at):
    rows = flat.shape[0] // cols
    shape = (rows, rows * cols)
    row = lax.broadcasted_iota(jnp.int32, shape, 0)
    position = lax.broadcasted_iota(jnp.int32, shape, 1)
    pick = jnp.where(position == row * cols + at, 1.0, 0.0).astype(BF16)
    return matmul(pick, flat).astype(BF16)


def fill_taps(taps, parts, row_halo, left, right, corners, rows, cols, chunk):
    width = taps.shape[1] // 3
    upper = lax.axis_index("gy") == 0
    for start in range(0, rows, chunk):
        count = chunk * cols
        begin = start * cols
        column = 0
        for part in parts:
            part_width = part.shape[1]
            value = part[pl.ds(begin, count), :]
            wide = value.astype(F32)
            where = column_of(wide.shape, cols)
            lanes = pl.ds(column, part_width)
            left_edge = spread(left[pl.ds(start, chunk), lanes], cols, 0)
            right_edge = spread(right[pl.ds(start, chunk), lanes], cols, cols - 1)
            before = jnp.where(where == 0, left_edge, pltpu.roll(wide, 1, axis=0))
            after = jnp.where(where == cols - 1, right_edge, pltpu.roll(wide, count - 1, axis=0))
            target = pl.ds(cols + begin, count)
            taps[target, pl.ds(column, part_width)] = before.astype(BF16)
            taps[target, pl.ds(width + column, part_width)] = value
            taps[target, pl.ds(2 * width + column, part_width)] = after.astype(BF16)
            column += part_width
    halo = row_halo[...].astype(F32)
    where = column_of(halo.shape, cols)
    first = jnp.broadcast_to(corners[pl.ds(0, 1), :].astype(F32), halo.shape)
    last = jnp.broadcast_to(corners[pl.ds(1, 1), :].astype(F32), halo.shape)
    before = jnp.where(where == 0, first, pltpu.roll(halo, 1, axis=0))
    after = jnp.where(where == cols - 1, last, pltpu.roll(halo, cols - 1, axis=0))
    for index, piece in enumerate((before, halo, after)):
        lanes = pl.ds(index * width, width)
        taps[pl.ds(0, cols), lanes] = jnp.where(upper, 0.0, piece).astype(BF16)
        taps[pl.ds((rows + 1) * cols, cols), lanes] = jnp.where(upper, piece, 0.0).astype(BF16)


def conv_chunk(taps, weights, begin, count, cols):
    total = matmul(taps[pl.ds(begin, count), :], weights[0])
    total = total + matmul(taps[pl.ds(begin + cols, count), :], weights[1])
    return total + matmul(taps[pl.ds(begin + 2 * cols, count), :], weights[2])


def lane_mean(value, low, size):
    return jnp.sum(jnp.where(low, value, 0.0), axis=-1, keepdims=True) / size


def step_forward(rows, cols, chunk):
    def body(radar, state, row_halo, left, right, corners, weights, bias, gain, state_grad,
             payload, sig_ref, mix_ref, cell_ref, taps):
        fill_taps(taps, (radar, state), row_halo, left, right, corners, rows, cols, chunk)
        count = chunk * cols
        half = state.shape[1] // 2
        for start in range(0, rows, chunk):
            begin = start * cols
            part = pl.ds(begin, count)
            gates = conv_chunk(taps, weights, begin, count, cols) + bias[...]
            low = low_half((count, 2 * half))
            sig = jax.nn.sigmoid(gates[:, : 2 * half])
            other = gates[:, 2 * half :]
            mix = jnp.where(low, jax.nn.sigmoid(other), jnp.tanh(other))
            held = state[part, :].astype(F32)
            terms = sig * jnp.where(low, swap_halves(mix), held)
            c_new = terms + swap_halves(terms)
            h_new = mix * jnp.tanh(c_new)
            inv_rms = lax.rsqrt(lane_mean(h_new * h_new, low, half) + EPS)
            normed = h_new * inv_rms * gain[...]
            grad = swap_halves(state_grad[part, :].astype(F32))
            payload[part, :] = jnp.where(low, normed, grad).astype(BF16)
            sig_ref[part, :] = sig
            mix_ref[part, :] = mix
            cell_ref[part, :] = jnp.where(low, h_new, c_new)

    return body


def attention(lines, length, block):
    def body(cells, w_rows, w_cols, w_mixed, w_q_back, w_kv_back, out,
             rows, grad_rows, cols, key_mask, value_mask, exps, probs, scores, mixed, grad_q, grad_kv):
        head = pl.program_id(1)
        size = w_rows.shape[1] // 4
        dim = size // HEADS
        scale = dim ** (-0.5)

        @pl.when(head == 0)
        def _():
            line = cells[...].reshape(length, cells.shape[-1])
            flat = matmul(line, w_rows[...]).astype(BF16)
            rows[:, pl.ds(0, 3 * size)] = flat[:, : 3 * size]
            rows[:, pl.ds(3 * size, size)] = jnp.ones((length, size), BF16)
            grad_rows[...] = flat[:, 3 * size :]
            cols[...] = matmul(w_cols[...], line, 1, 1).astype(BF16)
            mixed[...] = jnp.zeros_like(mixed)
            grad_q[...] = jnp.zeros_like(grad_q)

        key_mask[...] = jnp.zeros_like(key_mask)
        value_mask[...] = jnp.zeros_like(value_mask)
        at = pl.multiple_of(head * dim, dim)
        key_mask[pl.ds(at, dim), :] = cols[pl.ds(size + at, dim), :]
        value_mask[pl.ds(at, dim), :] = cols[pl.ds(2 * size + at, dim), :]
        lane = lax.broadcasted_iota(jnp.int32, (block, size), 1)
        mine = jnp.logical_and(lane >= at, lane < at + dim)
        total_v = jnp.zeros((dim, length), F32)
        total_k = jnp.zeros((dim, length), F32)
        for begin in range(0, length, block):
            part = pl.ds(begin, block)
            exps[part, :] = jnp.exp2(
                matmul(rows[part, pl.ds(0, size)], key_mask[...]) * (scale * LOG2E)
            ).astype(BF16)
            sums = matmul(exps[part, :], rows[:, pl.ds(2 * size, 2 * size)])
            inverse = 1.0 / sums[:, size:]
            attended = jnp.where(mine, sums[:, :size] * inverse, 0.0)
            mixed[part, :] += attended
            grads = grad_rows[part, :]
            inner = jnp.sum(attended * grads.astype(F32), axis=-1, keepdims=True)
            prob = exps[part, :].astype(F32) * inverse[:, :1]
            probs[part, :] = prob.astype(BF16)
            scores[part, :] = (
                prob * (matmul(grads, value_mask[...]) - inner)
            ).astype(BF16)
            grad_q[part, :] += jnp.where(
                mine, matmul(scores[part, :], rows[:, pl.ds(size, size)]), 0.0
            )
            total_v = total_v + matmul(
                cols[pl.ds(3 * size + at, dim), part], probs[part, :]
            )
            total_k = total_k + matmul(cols[pl.ds(at, dim), part], scores[part, :])
        grad_kv[pl.ds(at, dim), :] = (total_k * scale).astype(BF16)
        grad_kv[pl.ds(size + at, dim), :] = total_v.astype(BF16)

        @pl.when(head == HEADS - 1)
        def _():
            result = (
                matmul(mixed[...].astype(BF16), w_mixed[...])
                + matmul((grad_q[...] * scale).astype(BF16), w_q_back[...])
                + matmul(grad_kv[...], w_kv_back[...], 0, 0)
            )
            out[...] = result.astype(BF16).reshape(out.shape)

    return body


def attend(cells, w_rows, w_cols, w_mixed, w_q_back, w_kv_back):
    peers, lines, cols, width = cells.shape
    length = peers * cols
    size = w_mixed.shape[0]
    block = min(256, length)
    whole = lambda array: pl.BlockSpec(array.shape, lambda i, j: (0,) * array.ndim)
    line_spec = pl.BlockSpec((peers, None, cols, width), lambda i, j: (0, i, 0, 0))

    return pl.pallas_call(
        attention(lines, length, block),
        out_shape=jax.ShapeDtypeStruct(cells.shape, BF16),
        grid=(lines, HEADS),
        in_specs=[line_spec] + [whole(w) for w in (w_rows, w_cols, w_mixed, w_q_back, w_kv_back)],
        out_specs=line_spec,
        scratch_shapes=[
            pltpu.VMEM((length, 4 * size), BF16),
            pltpu.VMEM((length, size), BF16),
            pltpu.VMEM((4 * size, length), BF16),
            pltpu.VMEM((size, length), BF16),
            pltpu.VMEM((size, length), BF16),
            pltpu.VMEM((length, length), BF16),
            pltpu.VMEM((length, length), BF16),
            pltpu.VMEM((length, length), BF16),
            pltpu.VMEM((length, size), F32),
            pltpu.VMEM((length, size), F32),
            pltpu.VMEM((2 * size, length), BF16),
        ],
        compiler_params=pltpu.CompilerParams(
            dimension_semantics=("arbitrary", "arbitrary"), vmem_limit_bytes=48 << 20
        ),
    )(cells, w_rows, w_cols, w_mixed, w_q_back, w_kv_back)


def gate_grads(rows, cols, chunk):
    def body(back, state, state_grad, gain, sig_ref, mix_ref, cell_ref,
             new_state, grads, left, right, first, last, c_grad):
        count = chunk * cols
        half = state.shape[1] // 2
        for start in range(0, rows, chunk):
            part = pl.ds(start * cols, count)
            low = low_half((count, 2 * half))
            sig, mix, cell = sig_ref[part, :], mix_ref[part, :], cell_ref[part, :]
            arrived = back[part, :].astype(F32)
            new_state[part, :] = (cell + jnp.where(low, arrived, 0.0)).astype(BF16)
            held = state[part, :].astype(F32)
            given = state_grad[part, :].astype(F32)
            inv_rms = lax.rsqrt(lane_mean(cell * cell, low, half) + EPS)
            scaled = swap_halves(arrived) * gain[...]
            along = lane_mean(scaled * cell, low, half)
            hidden = given + inv_rms * scaled - cell * (inv_rms * inv_rms * inv_rms * along)
            hidden = jnp.where(low, hidden, swap_halves(hidden))
            c_new = jnp.where(low, swap_halves(cell), cell)
            c_tanh = jnp.tanh(c_new)
            mix_swapped = swap_halves(mix)
            out_gate = jnp.where(low, mix, mix_swapped)
            given_cell = jnp.where(low, swap_halves(given), given)
            cell_grad = given_cell + hidden * out_gate * (1.0 - c_tanh * c_tanh)
            one = cell_grad * jnp.where(low, mix_swapped, held) * sig * (1.0 - sig)
            two = jnp.where(
                low,
                hidden * c_tanh * mix * (1.0 - mix),
                cell_grad * swap_halves(sig) * (1.0 - mix * mix),
            )
            one, two = one.astype(BF16), two.astype(BF16)
            grads[part, pl.ds(0, 2 * half)] = one
            grads[part, pl.ds(2 * half, 2 * half)] = two
            c_grad[part, :] = (cell_grad * sig).astype(BF16)
            for lanes, value in ((pl.ds(0, 2 * half), one), (pl.ds(2 * half, 2 * half), two)):
                left[pl.ds(start, chunk), lanes] = pick_column(value, cols, 0)
                right[pl.ds(start, chunk), lanes] = pick_column(value, cols, cols - 1)
        first[...] = grads[pl.ds(0, cols), :]
        last[...] = grads[pl.ds((rows - 1) * cols, cols), :]

    return body


def step_backward(rows, cols, chunk):
    def body(grads, row_halo, left, right, corners, weights, c_grad, grad_frame, grad_state, taps):
        fill_taps(taps, (grads,), row_halo, left, right, corners, rows, cols, chunk)
        count = chunk * cols
        wide = grad_frame.shape[1]
        for start in range(0, rows, chunk):
            begin = start * cols
            part = pl.ds(begin, count)
            total = conv_chunk(taps, weights, begin, count, cols)
            grad_frame[part, :] = total[:, :wide].astype(BF16)
            rest = total[:, wide:].astype(BF16)
            grad_state[part, :] = jnp.where(low_half(rest.shape), rest, c_grad[part, :])

    return body


def exchange(first_col, last_col, first_row, last_row):
    count = lax.axis_size("gx")
    forward = [(i, i + 1) for i in range(count - 1)]
    backward = [(target, source) for source, target in forward]
    left = lax.ppermute(last_col, "gx", forward)
    right = lax.ppermute(first_col, "gx", backward)
    border = jnp.where(lax.axis_index("gy") == 0, last_row, first_row)
    row_halo = lax.ppermute(border, "gy", [(0, 1), (1, 0)])
    across = lambda pairs: [
        (y * count + source, (1 - y) * count + target) for y in (0, 1) for source, target in pairs
    ]
    low = lax.ppermute(border[-1:], ("gy", "gx"), across(forward))
    high = lax.ppermute(border[:1], ("gy", "gx"), across(backward))
    return row_halo, left, right, jnp.concatenate([low, high], axis=0)


def on_device(radar_frame, lstm_state, w_conv, b_gates, norm_gain, w_qkv, w_out, state_grad):
    row_count, col_count, in_channels = radar_frame.shape
    hidden = lstm_state.shape[2] // 2
    gate_dim = w_conv.shape[3]
    attn_dim = w_out.shape[0]
    cells = row_count * col_count
    chunk = min(32, row_count)
    lines = row_count // lax.axis_size("gx")
    shape = lambda *dims: jax.ShapeDtypeStruct(dims, BF16)
    wide = lambda *dims: jax.ShapeDtypeStruct(dims, F32)
    vmem = pltpu.VMEM

    radar = radar_frame.reshape(cells, in_channels)
    state = lstm_state.reshape(cells, 2 * hidden)
    given = state_grad.reshape(cells, 2 * hidden)
    both = lambda a, b: jnp.concatenate([a, b], axis=-1)
    halo = exchange(
        both(radar_frame[:, 0], lstm_state[:, 0]),
        both(radar_frame[:, -1], lstm_state[:, -1]),
        both(radar_frame[0], lstm_state[0]),
        both(radar_frame[-1], lstm_state[-1]),
    )
    in_pad = 2 * hidden + in_channels - w_conv.shape[2]
    padded = jnp.pad(w_conv, ((0, 0), (0, 0), (0, in_pad), (0, 0)))
    w_forward = padded.reshape(3, -1, gate_dim)
    w_backward = padded[::-1, ::-1].transpose(0, 1, 3, 2).reshape(3, 3 * gate_dim, -1)
    gain = jnp.tile(norm_gain, 2)[None]

    payload, sig, mix, cell = call(
        step_forward(row_count, col_count, chunk),
        (shape(cells, 2 * hidden),) + (wide(cells, 2 * hidden),) * 3,
        [vmem(((row_count + 2) * col_count, 3 * (in_channels + 2 * hidden)), BF16)],
    )(radar, state, *halo, w_forward, b_gates[None], gain, given)

    peers = lax.axis_size("gx")
    send = payload.reshape(peers, lines, col_count, 2 * hidden)
    lines_in = lax.all_to_all(send, "gx", split_axis=0, concat_axis=0, tiled=True)
    none = jnp.zeros((hidden, attn_dim), BF16)
    w_qkv_down = jnp.concatenate([w_qkv, jnp.zeros_like(w_qkv)], axis=0)
    w_grad_down = jnp.concatenate([none, w_out.T], axis=0)
    w_all = jnp.concatenate([w_qkv_down, w_grad_down], axis=1)
    w_mixed = jnp.concatenate([w_out, jnp.zeros_like(w_out)], axis=1)
    w_back = jnp.concatenate([jnp.zeros_like(w_qkv), w_qkv], axis=0).T
    lines_out = attend(
        lines_in, w_all, w_all.T, w_mixed, w_back[:attn_dim], w_back[attn_dim:]
    )
    back = lax.all_to_all(lines_out, "gx", split_axis=0, concat_axis=0, tiled=True)

    new_state, grads, left, right, first, last, c_grad = call(
        gate_grads(row_count, col_count, chunk),
        (
            shape(cells, 2 * hidden),
            shape(cells, gate_dim),
            shape(row_count, gate_dim),
            shape(row_count, gate_dim),
            shape(col_count, gate_dim),
            shape(col_count, gate_dim),
            shape(cells, 2 * hidden),
        ),
    )(back.reshape(cells, 2 * hidden), state, given, gain, sig, mix, cell)
    halo = exchange(left, right, first, last)
    grad_frame, grad_state = call(
        step_backward(row_count, col_count, chunk),
        (shape(cells, in_channels), shape(cells, 2 * hidden)),
        [vmem(((row_count + 2) * col_count, 3 * gate_dim), BF16)],
    )(grads, *halo, w_backward, c_grad)
    whole = lambda array: array.reshape(row_count, col_count, -1)
    return whole(new_state), whole(grad_frame), whole(grad_state)


def solution(mesh):
    spec = P("gy", "gx", None)
    return jax.shard_map(
        on_device,
        mesh=mesh,
        in_specs=(spec, spec, P(), P(), P(), P(), P(), spec),
        out_specs=(spec, spec, spec),
        check_vma=False,
    )
```

```python
import jax
import jax.numpy as jnp
from jax import lax
from jax.experimental import pallas as pl
from jax.experimental.pallas import tpu as pltpu
from jax.sharding import PartitionSpec as P

HEADS = 8
EPS = 1e-05
LOG2E = 1.4426950408889634
VMEM_ATTEND = 28
F32 = jnp.float32
BF16 = jnp.bfloat16


def matmul(lhs, rhs, lhs_dim=1, rhs_dim=0):
    return lax.dot_general(
        lhs, rhs, (((lhs_dim,), (rhs_dim,)), ((), ())), preferred_element_type=F32
    )


def call(body, out_shape, scratch=(), vmem=24):
    return pl.pallas_call(
        body,
        out_shape=out_shape,
        scratch_shapes=list(scratch),
        compiler_params=pltpu.CompilerParams(vmem_limit_bytes=vmem << 20),
    )


def low_half(shape):
    return lax.broadcasted_iota(jnp.int32, shape, 1) < shape[1] // 2


def swap_halves(value):
    return pltpu.roll(value, value.shape[1] // 2, axis=1)


def column_of(shape, cols):
    return lax.rem(lax.broadcasted_iota(jnp.int32, shape, 0), cols)


def spread(edge, cols, at):
    rows = edge.shape[0]
    shape = (rows * cols, rows)
    position = lax.broadcasted_iota(jnp.int32, shape, 0)
    row = lax.broadcasted_iota(jnp.int32, shape, 1)
    pick = jnp.where(position == row * cols + at, 1.0, 0.0).astype(BF16)
    return matmul(pick, edge)


def pick_column(flat, cols, at):
    rows = flat.shape[0] // cols
    shape = (rows, rows * cols)
    row = lax.broadcasted_iota(jnp.int32, shape, 0)
    position = lax.broadcasted_iota(jnp.int32, shape, 1)
    pick = jnp.where(position == row * cols + at, 1.0, 0.0).astype(BF16)
    return matmul(pick, flat).astype(BF16)


def fill_taps(taps, parts, row_halo, left, right, rows, cols, chunk):
    width = taps.shape[1] // 3
    upper = lax.axis_index("gy") == 0
    for start in range(0, rows, chunk):
        count = chunk * cols
        begin = start * cols
        column = 0
        for part in parts:
            part_width = part.shape[1]
            value = part[pl.ds(begin, count), :]
            wide = value.astype(F32)
            where = column_of(wide.shape, cols)
            lanes = pl.ds(column, part_width)
            left_edge = spread(left[pl.ds(start, chunk), lanes], cols, 0)
            right_edge = spread(right[pl.ds(start, chunk), lanes], cols, cols - 1)
            before = jnp.where(where == 0, left_edge, pltpu.roll(wide, 1, axis=0))
            after = jnp.where(where == cols - 1, right_edge, pltpu.roll(wide, count - 1, axis=0))
            target = pl.ds(cols + begin, count)
            taps[target, pl.ds(column, part_width)] = before.astype(BF16)
            taps[target, pl.ds(width + column, part_width)] = value
            taps[target, pl.ds(2 * width + column, part_width)] = after.astype(BF16)
            column += part_width
    halo = row_halo[pl.ds(0, cols), :].astype(F32)
    where = column_of(halo.shape, cols)
    first = jnp.broadcast_to(row_halo[pl.ds(cols, 1), :].astype(F32), halo.shape)
    last = jnp.broadcast_to(row_halo[pl.ds(cols + 1, 1), :].astype(F32), halo.shape)
    before = jnp.where(where == 0, first, pltpu.roll(halo, 1, axis=0))
    after = jnp.where(where == cols - 1, last, pltpu.roll(halo, cols - 1, axis=0))
    for index, piece in enumerate((before, halo, after)):
        lanes = pl.ds(index * width, width)
        taps[pl.ds(0, cols), lanes] = jnp.where(upper, 0.0, piece).astype(BF16)
        taps[pl.ds((rows + 1) * cols, cols), lanes] = jnp.where(upper, piece, 0.0).astype(BF16)


def conv_forward(taps, w_conv, begin, count, cols):
    depth = w_conv.shape[2]
    width = taps.shape[1] // 3
    total = None
    for row_tap in range(3):
        for col_tap in range(3):
            window = taps[pl.ds(begin + row_tap * cols, count), pl.ds(col_tap * width, depth)]
            term = matmul(window, w_conv[row_tap, col_tap])
            total = term if total is None else total + term
    return total


def conv_backward(taps, w_conv, begin, count, cols):
    width = taps.shape[1] // 3
    total = None
    for row_tap in range(3):
        for col_tap in range(3):
            window = taps[pl.ds(begin + row_tap * cols, count), pl.ds(col_tap * width, width)]
            term = matmul(window, w_conv[2 - row_tap, 2 - col_tap], 1, 1)
            total = term if total is None else total + term
    return total


def lane_mean(value, low, size):
    return jnp.sum(jnp.where(low, value, 0.0), axis=-1, keepdims=True) / size


def edges(rows, cols, chunk):
    def body(radar, state, left, right, first, last):
        width = radar.shape[1]
        for part, lanes in ((radar, pl.ds(0, width)), (state, pl.ds(width, state.shape[1]))):
            for start in range(0, rows, chunk):
                value = part[pl.ds(start * cols, chunk * cols), :]
                left[pl.ds(start, chunk), lanes] = pick_column(value, cols, 0)
                right[pl.ds(start, chunk), lanes] = pick_column(value, cols, cols - 1)
            first[:, lanes] = part[pl.ds(0, cols), :]
            last[:, lanes] = part[pl.ds((rows - 1) * cols, cols), :]

    return body


def step_forward(rows, cols, chunk):
    def body(radar, state, row_halo, left, right, weights, bias, gain, state_grad,
             payload, sig_ref, mix_ref, cell_ref, taps):
        fill_taps(taps, (radar, state), row_halo, left, right, rows, cols, chunk)
        count = chunk * cols
        half = state.shape[1] // 2
        for start in range(0, rows, chunk):
            begin = start * cols
            part = pl.ds(begin, count)
            gates = conv_forward(taps, weights, begin, count, cols) + bias[...]
            low = low_half((count, 2 * half))
            sig = jax.nn.sigmoid(gates[:, : 2 * half])
            other = gates[:, 2 * half :]
            mix = jnp.where(low, jax.nn.sigmoid(other), jnp.tanh(other))
            held = state[part, :].astype(F32)
            terms = sig * jnp.where(low, swap_halves(mix), held)
            c_new = terms + swap_halves(terms)
            h_new = mix * jnp.tanh(c_new)
            inv_rms = lax.rsqrt(lane_mean(h_new * h_new, low, half) + EPS)
            normed = h_new * inv_rms * jnp.concatenate([gain[...], gain[...]], axis=1)
            grad = swap_halves(state_grad[part, :].astype(F32))
            payload[part, :] = jnp.where(low, normed, grad).astype(BF16)
            sig_ref[part, :] = sig
            mix_ref[part, :] = mix
            cell_ref[part, :] = jnp.where(low, h_new, c_new)

    return body


def attention(length, block):
    def body(cells, w_qkv, w_out_t, out, w_qkv_t, rows, cols, query_mask, grad_mask, values, exps, probs,
             scores, mixed, grad_q, grad_k, grad_v):
        head = pl.program_id(1)
        size = w_out_t.shape[1]
        dim = size // HEADS
        scale = dim ** (-0.5)

        @pl.when(head == 0)
        def _():
            line = cells[...].reshape(length, cells.shape[-1]).astype(F32)
            half = line.shape[1] // 2
            normed = line[:, :half].astype(BF16)
            given = swap_halves(line)[:, :half].astype(BF16)
            w_qkv_t[...] = w_qkv[...].astype(F32).T.astype(BF16)
            w_out = w_out_t[...].astype(F32).T.astype(BF16)
            rows[...] = matmul(normed, w_qkv[:, pl.ds(size, 2 * size)]).astype(BF16)
            cols[pl.ds(0, 3 * size), :] = matmul(w_qkv_t[...], normed, 1, 1).astype(BF16)
            cols[pl.ds(3 * size, size), :] = matmul(w_out, given, 1, 1).astype(BF16)
            values[pl.ds(dim, dim), :] = jnp.ones((dim, length), BF16)

        at = pl.multiple_of(head * dim, dim)
        mine = pl.ds(at, dim)
        query_cols = cols[mine, :]
        key_cols = cols[pl.ds(size + at, dim), :]
        grad_cols = cols[pl.ds(3 * size + at, dim), :]
        query_mask[...] = jnp.zeros_like(query_mask)
        grad_mask[...] = jnp.zeros_like(grad_mask)
        query_mask[mine, :] = query_cols
        grad_mask[mine, :] = grad_cols
        values[pl.ds(0, dim), :] = cols[pl.ds(2 * size + at, dim), :]
        for begin in range(0, length, block):
            part = pl.ds(begin, block)
            exps[:, part] = jnp.exp2(
                matmul(rows[:, pl.ds(0, size)], query_mask[:, part]) * (scale * LOG2E)
            ).astype(BF16)
            sums = matmul(values[...], exps[:, part])
            inverse = 1.0 / sums[dim : dim + 1]
            attended = sums[:dim] * inverse
            mixed[mine, part] = attended.astype(BF16)
            grads = cols[pl.ds(3 * size + at, dim), part].astype(F32)
            inner = jnp.sum(attended * grads, axis=0, keepdims=True)
            prob = exps[:, part].astype(F32) * inverse
            probs[:, part] = prob.astype(BF16)
            grad_prob = matmul(rows[:, pl.ds(size, size)], grad_mask[:, part])
            scores[:, part] = (prob * (grad_prob - inner)).astype(BF16)
            grad_q[mine, part] = (matmul(key_cols, scores[:, part]) * scale).astype(BF16)
        grad_k[mine, :] = (matmul(query_cols, scores[...], 1, 1) * scale).astype(BF16)
        grad_v[mine, :] = matmul(grad_cols, probs[...], 1, 1).astype(BF16)

        @pl.when(head == HEADS - 1)
        def _():
            w_out = w_out_t[...].astype(F32).T.astype(BF16)
            back = (
                matmul(grad_q[...], w_qkv_t[pl.ds(0, size), :], 0, 0)
                + matmul(grad_k[...], w_qkv_t[pl.ds(size, size), :], 0, 0)
                + matmul(grad_v[...], w_qkv_t[pl.ds(2 * size, size), :], 0, 0)
            )
            result = jnp.concatenate([matmul(mixed[...], w_out, 0, 0), back], axis=1)
            out[...] = result.astype(BF16).reshape(out.shape)

    return body


def attend(cells, w_qkv, w_out_t):
    peers, lines, cols, width = cells.shape
    length = peers * cols
    size = w_out_t.shape[1]
    block = min(512, length)
    whole = lambda array: pl.BlockSpec(array.shape, lambda i, j: (0,) * array.ndim)
    line_spec = pl.BlockSpec((peers, None, cols, width), lambda i, j: (0, i, 0, 0))
    tall = pltpu.VMEM((size, length), BF16)
    square = pltpu.VMEM((length, length), BF16)
    return pl.pallas_call(
        attention(length, block),
        out_shape=jax.ShapeDtypeStruct(cells.shape, BF16),
        grid=(lines, HEADS),
        in_specs=[line_spec, whole(w_qkv), whole(w_out_t)],
        out_specs=line_spec,
        scratch_shapes=[
            pltpu.VMEM(w_qkv.shape[::-1], BF16),
            pltpu.VMEM((length, 2 * size), BF16),
            pltpu.VMEM((4 * size, length), BF16),
            tall,
            tall,
            pltpu.VMEM((2 * size // HEADS, length), BF16),
            square,
            square,
            square,
            tall,
            tall,
            tall,
            tall,
        ],
        compiler_params=pltpu.CompilerParams(
            dimension_semantics=("arbitrary", "arbitrary"), vmem_limit_bytes=VMEM_ATTEND << 20
        ),
    )(cells, w_qkv, w_out_t)


def gate_grads(rows, cols, chunk):
    def body(back, state, state_grad, gain, sig_ref, mix_ref, cell_ref,
             new_state, grads, left, right, first, last, c_grad):
        count = chunk * cols
        half = state.shape[1] // 2
        for start in range(0, rows, chunk):
            part = pl.ds(start * cols, count)
            low = low_half((count, 2 * half))
            sig, mix, cell = sig_ref[part, :], mix_ref[part, :], cell_ref[part, :]
            arrived = back[part, :].astype(F32)
            new_state[part, :] = (cell + jnp.where(low, arrived, 0.0)).astype(BF16)
            held = state[part, :].astype(F32)
            given = state_grad[part, :].astype(F32)
            inv_rms = lax.rsqrt(lane_mean(cell * cell, low, half) + EPS)
            scaled = swap_halves(arrived) * jnp.concatenate([gain[...], gain[...]], axis=1)
            along = lane_mean(scaled * cell, low, half)
            hidden = given + inv_rms * scaled - cell * (inv_rms * inv_rms * inv_rms * along)
            hidden = jnp.where(low, hidden, swap_halves(hidden))
            c_new = jnp.where(low, swap_halves(cell), cell)
            c_tanh = jnp.tanh(c_new)
            mix_swapped = swap_halves(mix)
            out_gate = jnp.where(low, mix, mix_swapped)
            given_cell = jnp.where(low, swap_halves(given), given)
            cell_grad = given_cell + hidden * out_gate * (1.0 - c_tanh * c_tanh)
            one = cell_grad * jnp.where(low, mix_swapped, held) * sig * (1.0 - sig)
            two = jnp.where(
                low,
                hidden * c_tanh * mix * (1.0 - mix),
                cell_grad * swap_halves(sig) * (1.0 - mix * mix),
            )
            one, two = one.astype(BF16), two.astype(BF16)
            grads[part, pl.ds(0, 2 * half)] = one
            grads[part, pl.ds(2 * half, 2 * half)] = two
            c_grad[part, :] = (cell_grad * sig).astype(BF16)
            for lanes, value in ((pl.ds(0, 2 * half), one), (pl.ds(2 * half, 2 * half), two)):
                left[pl.ds(start, chunk), lanes] = pick_column(value, cols, 0)
                right[pl.ds(start, chunk), lanes] = pick_column(value, cols, cols - 1)
        first[...] = grads[pl.ds(0, cols), :]
        last[...] = grads[pl.ds((rows - 1) * cols, cols), :]

    return body


def step_backward(rows, cols, chunk):
    def body(grads, row_halo, left, right, weights, c_grad, grad_frame, grad_state, taps):
        fill_taps(taps, (grads,), row_halo, left, right, rows, cols, chunk)
        count = chunk * cols
        wide = grad_frame.shape[1]
        for start in range(0, rows, chunk):
            begin = start * cols
            part = pl.ds(begin, count)
            total = conv_backward(taps, weights, begin, count, cols).astype(BF16)
            rest = total.shape[1] - wide
            grad_frame[part, :] = total[:, :wide]
            grad_state[part, pl.ds(0, rest)] = total[:, wide:]
            grad_state[part, pl.ds(rest, rest)] = c_grad[part, pl.ds(rest, rest)]

    return body


def exchange(first_col, last_col, first_row, last_row):
    count = lax.axis_size("gx")
    forward = [(i, i + 1) for i in range(count - 1)]
    backward = [(target, source) for source, target in forward]
    left = lax.ppermute(last_col, "gx", forward)
    right = lax.ppermute(first_col, "gx", backward)
    upper = lax.axis_index("gy") == 0
    border = jnp.where(upper, last_row, first_row)
    edge = lambda column: jnp.where(upper, column[-1:], column[:1])
    sent = jnp.concatenate([border, edge(left), edge(right)], axis=0)
    received = lax.ppermute(sent, "gy", [(0, 1), (1, 0)])
    return received, left, right


def on_device(radar_frame, lstm_state, w_conv, b_gates, norm_gain, w_qkv, w_out, state_grad):
    row_count, col_count, in_channels = radar_frame.shape
    hidden = lstm_state.shape[2] // 2
    gate_dim = w_conv.shape[3]
    attn_dim = w_out.shape[0]
    cells = row_count * col_count
    chunk = min(32, row_count)
    lines = row_count // lax.axis_size("gx")
    shape = lambda *dims: jax.ShapeDtypeStruct(dims, BF16)
    wide = lambda *dims: jax.ShapeDtypeStruct(dims, F32)
    vmem = pltpu.VMEM

    radar = radar_frame.reshape(cells, in_channels)
    state = lstm_state.reshape(cells, 2 * hidden)
    given = state_grad.reshape(cells, 2 * hidden)
    depth = in_channels + 2 * hidden
    sides = call(
        edges(row_count, col_count, chunk),
        (shape(row_count, depth),) * 2 + (shape(col_count, depth),) * 2,
    )(radar, state)
    halo = exchange(*sides)
    gain = norm_gain[None]

    payload, sig, mix, cell = call(
        step_forward(row_count, col_count, chunk),
        (shape(cells, 2 * hidden),) + (wide(cells, 2 * hidden),) * 3,
        [vmem(((row_count + 2) * col_count, 3 * (in_channels + 2 * hidden)), BF16)],
    )(radar, state, *halo, w_conv, b_gates[None], gain, given)

    peers = lax.axis_size("gx")
    send = payload.reshape(peers, lines, col_count, 2 * hidden)
    lines_in = lax.all_to_all(send, "gx", split_axis=0, concat_axis=0, tiled=True)
    lines_out = attend(lines_in, w_qkv, w_out.T)
    back = lax.all_to_all(lines_out, "gx", split_axis=0, concat_axis=0, tiled=True)

    new_state, grads, left, right, first, last, c_grad = call(
        gate_grads(row_count, col_count, chunk),
        (
            shape(cells, 2 * hidden),
            shape(cells, gate_dim),
            shape(row_count, gate_dim),
            shape(row_count, gate_dim),
            shape(col_count, gate_dim),
            shape(col_count, gate_dim),
            shape(cells, 2 * hidden),
        ),
    )(back.reshape(cells, 2 * hidden), state, given, gain, sig, mix, cell)
    halo = exchange(left, right, first, last)
    grad_frame, grad_state = call(
        step_backward(row_count, col_count, chunk),
        (shape(cells, in_channels), shape(cells, 2 * hidden)),
        [vmem(((row_count + 2) * col_count, 3 * gate_dim), BF16)],
    )(grads, *halo, w_conv, c_grad)
    whole = lambda array: array.reshape(row_count, col_count, -1)
    return whole(new_state), whole(grad_frame), whole(grad_state)


def solution(mesh):
    spec = P("gy", "gx", None)
    return jax.shard_map(
        on_device,
        mesh=mesh,
        in_specs=(spec, spec, P(), P(), P(), P(), P(), spec),
        out_specs=(spec, spec, spec),
        check_vma=False,
    )
```

```python
import jax
import jax.numpy as jnp
from jax import lax
from jax.experimental import pallas as pl
from jax.experimental.pallas import tpu as pltpu
from jax.sharding import PartitionSpec as P

HEADS = 8
EPS = 1e-05
LOG2E = 1.4426950408889634
VMEM_ATTEND = 28
F32 = jnp.float32
BF16 = jnp.bfloat16


def matmul(lhs, rhs, lhs_dim=1, rhs_dim=0):
    return lax.dot_general(
        lhs, rhs, (((lhs_dim,), (rhs_dim,)), ((), ())), preferred_element_type=F32
    )


def call(body, out_shape, scratch=(), in_place=(), count=0, vmem=24):
    spaces = [pltpu.HBM if index in in_place else pltpu.VMEM for index in range(count)]
    return pl.pallas_call(
        body,
        out_shape=out_shape,
        in_specs=[pl.BlockSpec(memory_space=space) for space in spaces],
        scratch_shapes=list(scratch),
        compiler_params=pltpu.CompilerParams(vmem_limit_bytes=vmem << 20),
    )


def low_half(shape):
    return lax.broadcasted_iota(jnp.int32, shape, 1) < shape[1] // 2


def swap_halves(value):
    return pltpu.roll(value, value.shape[1] // 2, axis=1)


def column_of(shape, cols):
    return lax.rem(lax.broadcasted_iota(jnp.int32, shape, 0), cols)


def spread(edge, cols, at):
    rows = edge.shape[0]
    shape = (rows * cols, rows)
    position = lax.broadcasted_iota(jnp.int32, shape, 0)
    row = lax.broadcasted_iota(jnp.int32, shape, 1)
    pick = jnp.where(position == row * cols + at, 1.0, 0.0).astype(BF16)
    return matmul(pick, edge)


def pick_column(flat, cols, at):
    rows = flat.shape[0] // cols
    shape = (rows, rows * cols)
    row = lax.broadcasted_iota(jnp.int32, shape, 0)
    position = lax.broadcasted_iota(jnp.int32, shape, 1)
    pick = jnp.where(position == row * cols + at, 1.0, 0.0).astype(BF16)
    return matmul(pick, flat).astype(BF16)


def fill_taps(taps, parts, row_halo, left, right, rows, cols, chunk):
    width = taps.shape[1] // 3
    upper = lax.axis_index("gy") == 0
    for start in range(0, rows, chunk):
        count = chunk * cols
        begin = start * cols
        column = 0
        for part in parts:
            part_width = part.shape[1]
            value = part[pl.ds(begin, count), :]
            wide = value.astype(F32)
            where = column_of(wide.shape, cols)
            lanes = pl.ds(column, part_width)
            left_edge = spread(left[pl.ds(start, chunk), lanes], cols, 0)
            right_edge = spread(right[pl.ds(start, chunk), lanes], cols, cols - 1)
            before = jnp.where(where == 0, left_edge, pltpu.roll(wide, 1, axis=0))
            after = jnp.where(where == cols - 1, right_edge, pltpu.roll(wide, count - 1, axis=0))
            target = pl.ds(cols + begin, count)
            taps[target, pl.ds(column, part_width)] = before.astype(BF16)
            taps[target, pl.ds(width + column, part_width)] = value
            taps[target, pl.ds(2 * width + column, part_width)] = after.astype(BF16)
            column += part_width
    halo = row_halo[...].astype(F32)
    where = column_of(halo.shape, cols)
    first = jnp.broadcast_to(left[pl.ds(rows, 1), :].astype(F32), halo.shape)
    last = jnp.broadcast_to(right[pl.ds(rows, 1), :].astype(F32), halo.shape)
    before = jnp.where(where == 0, first, pltpu.roll(halo, 1, axis=0))
    after = jnp.where(where == cols - 1, last, pltpu.roll(halo, cols - 1, axis=0))
    for index, piece in enumerate((before, halo, after)):
        lanes = pl.ds(index * width, width)
        taps[pl.ds(0, cols), lanes] = jnp.where(upper, 0.0, piece).astype(BF16)
        taps[pl.ds((rows + 1) * cols, cols), lanes] = jnp.where(upper, piece, 0.0).astype(BF16)


def conv_forward(taps, w_conv, begin, count, cols):
    depth = w_conv.shape[2]
    width = taps.shape[1] // 3
    total = None
    for row_tap in range(3):
        for col_tap in range(3):
            window = taps[pl.ds(begin + row_tap * cols, count), pl.ds(col_tap * width, depth)]
            term = matmul(window, w_conv[row_tap, col_tap])
            total = term if total is None else total + term
    return total


def conv_backward(taps, w_conv, begin, count, cols):
    width = taps.shape[1] // 3
    total = None
    for row_tap in range(3):
        for col_tap in range(3):
            window = taps[pl.ds(begin + row_tap * cols, count), pl.ds(col_tap * width, width)]
            term = matmul(window, w_conv[2 - row_tap, 2 - col_tap], 1, 1)
            total = term if total is None else total + term
    return total


def lane_mean(value, low, size):
    return jnp.sum(jnp.where(low, value, 0.0), axis=-1, keepdims=True) / size


def fetch(source, target, sems, pieces):
    size = source.shape[0] // pieces
    copies = [
        pltpu.make_async_copy(
            source.at[pl.ds(index * size, size)], target.at[pl.ds(index * size, size)], sems.at[index]
        )
        for index in range(pieces)
    ]
    for copy in copies:
        copy.start()
    return copies


def edges(rows, cols, chunk):
    pieces = rows // chunk

    def body(radar, state, bias_in, gain_in, left, right, radar_here, state_here, bias, gain,
             radar_sems, state_sems, sems):
        small = (
            pltpu.make_async_copy(bias_in, bias, sems.at[0]),
            pltpu.make_async_copy(gain_in, gain, sems.at[1]),
        )
        ready = (
            fetch(radar, radar_here, radar_sems, pieces),
            fetch(state, state_here, state_sems, pieces),
        )
        for copy in small:
            copy.start()
        width = radar.shape[1]
        for index in range(pieces):
            for part, copies, lanes in (
                (radar_here, ready[0], pl.ds(0, width)),
                (state_here, ready[1], pl.ds(width, state.shape[1])),
            ):
                copies[index].wait()
                value = part[pl.ds(index * chunk * cols, chunk * cols), :]
                left[pl.ds(index * chunk, chunk), lanes] = pick_column(value, cols, 0)
                right[pl.ds(index * chunk, chunk), lanes] = pick_column(value, cols, cols - 1)
        for copy in small:
            copy.wait()

    return body


def step_forward(rows, cols, chunk):
    def body(radar, state, row_halo, left, right, weights_out, bias, gain, grad_out,
             payload, sig_ref, mix_ref, cell_ref, taps, weights, state_grad, sems, grad_sems):
        later = fetch(weights_out, weights, sems, 3) + fetch(grad_out, state_grad, grad_sems, 1)
        fill_taps(taps, (radar, state), row_halo, left, right, rows, cols, chunk)
        for copy in later:
            copy.wait()
        count = chunk * cols
        half = state.shape[1] // 2
        for start in range(0, rows, chunk):
            begin = start * cols
            part = pl.ds(begin, count)
            gates = conv_forward(taps, weights, begin, count, cols) + bias[...]
            low = low_half((count, 2 * half))
            sig = jax.nn.sigmoid(gates[:, : 2 * half])
            other = gates[:, 2 * half :]
            mix = jnp.where(low, jax.nn.sigmoid(other), jnp.tanh(other))
            held = state[part, :].astype(F32)
            terms = sig * jnp.where(low, swap_halves(mix), held)
            c_new = terms + swap_halves(terms)
            h_new = mix * jnp.tanh(c_new)
            inv_rms = lax.rsqrt(lane_mean(h_new * h_new, low, half) + EPS)
            normed = h_new * inv_rms * jnp.concatenate([gain[...], gain[...]], axis=1)
            grad = swap_halves(state_grad[part, :].astype(F32))
            payload[part, :] = jnp.where(low, normed, grad).astype(BF16)
            sig_ref[part, :] = sig
            mix_ref[part, :] = mix
            cell_ref[part, :] = jnp.where(low, h_new, c_new)

    return body


def attention(length, block):
    def body(cells, w_qkv, w_out_t, out, w_qkv_t, rows, cols, query_mask, grad_mask, values, exps, probs,
             scores, mixed, grad_q, grad_k, grad_v):
        head = pl.program_id(1)
        size = w_out_t.shape[1]
        dim = size // HEADS
        scale = dim ** (-0.5)

        @pl.when(head == 0)
        def _():
            line = cells[...].reshape(length, cells.shape[-1]).astype(F32)
            half = line.shape[1] // 2
            normed = line[:, :half].astype(BF16)
            given = swap_halves(line)[:, :half].astype(BF16)
            w_qkv_t[...] = w_qkv[...].astype(F32).T.astype(BF16)
            w_out = w_out_t[...].astype(F32).T.astype(BF16)
            rows[...] = matmul(normed, w_qkv[:, pl.ds(size, 2 * size)]).astype(BF16)
            cols[pl.ds(0, 3 * size), :] = matmul(w_qkv_t[...], normed, 1, 1).astype(BF16)
            cols[pl.ds(3 * size, size), :] = matmul(w_out, given, 1, 1).astype(BF16)
            values[pl.ds(dim, dim), :] = jnp.ones((dim, length), BF16)

        at = pl.multiple_of(head * dim, dim)
        mine = pl.ds(at, dim)
        query_cols = cols[mine, :]
        key_cols = cols[pl.ds(size + at, dim), :]
        grad_cols = cols[pl.ds(3 * size + at, dim), :]
        query_mask[...] = jnp.zeros_like(query_mask)
        grad_mask[...] = jnp.zeros_like(grad_mask)
        query_mask[mine, :] = query_cols
        grad_mask[mine, :] = grad_cols
        values[pl.ds(0, dim), :] = cols[pl.ds(2 * size + at, dim), :]
        for begin in range(0, length, block):
            part = pl.ds(begin, block)
            exps[:, part] = jnp.exp2(
                matmul(rows[:, pl.ds(0, size)], query_mask[:, part]) * (scale * LOG2E)
            ).astype(BF16)
            sums = matmul(values[...], exps[:, part])
            inverse = 1.0 / sums[dim : dim + 1]
            attended = sums[:dim] * inverse
            mixed[mine, part] = attended.astype(BF16)
            grads = cols[pl.ds(3 * size + at, dim), part].astype(F32)
            inner = jnp.sum(attended * grads, axis=0, keepdims=True)
            prob = exps[:, part] * inverse.astype(BF16)
            probs[:, part] = prob
            grad_prob = matmul(rows[:, pl.ds(size, size)], grad_mask[:, part])
            scores[:, part] = prob * (grad_prob - inner).astype(BF16)
            grad_q[mine, part] = (matmul(key_cols, scores[:, part]) * scale).astype(BF16)
        grad_k[mine, :] = (matmul(query_cols, scores[...], 1, 1) * scale).astype(BF16)
        grad_v[mine, :] = matmul(grad_cols, probs[...], 1, 1).astype(BF16)

        @pl.when(head == HEADS - 1)
        def _():
            w_out = w_out_t[...].astype(F32).T.astype(BF16)
            back = (
                matmul(grad_q[...], w_qkv_t[pl.ds(0, size), :], 0, 0)
                + matmul(grad_k[...], w_qkv_t[pl.ds(size, size), :], 0, 0)
                + matmul(grad_v[...], w_qkv_t[pl.ds(2 * size, size), :], 0, 0)
            )
            result = jnp.concatenate([matmul(mixed[...], w_out, 0, 0), back], axis=1)
            out[...] = result.astype(BF16).reshape(out.shape)

    return body


def attend(cells, w_qkv, w_out_t):
    peers, lines, cols, width = cells.shape
    length = peers * cols
    size = w_out_t.shape[1]
    block = min(512, length)
    whole = lambda array: pl.BlockSpec(array.shape, lambda i, j: (0,) * array.ndim)
    line_spec = pl.BlockSpec((peers, None, cols, width), lambda i, j: (0, i, 0, 0))
    tall = pltpu.VMEM((size, length), BF16)
    square = pltpu.VMEM((length, length), BF16)
    return pl.pallas_call(
        attention(length, block),
        out_shape=jax.ShapeDtypeStruct(cells.shape, BF16),
        grid=(lines, HEADS),
        in_specs=[line_spec, whole(w_qkv), whole(w_out_t)],
        out_specs=line_spec,
        scratch_shapes=[
            pltpu.VMEM(w_qkv.shape[::-1], BF16),
            pltpu.VMEM((length, 2 * size), BF16),
            pltpu.VMEM((4 * size, length), BF16),
            tall,
            tall,
            pltpu.VMEM((2 * size // HEADS, length), BF16),
            square,
            square,
            square,
            tall,
            tall,
            tall,
            tall,
        ],
        compiler_params=pltpu.CompilerParams(
            dimension_semantics=("arbitrary", "arbitrary"), vmem_limit_bytes=VMEM_ATTEND << 20
        ),
    )(cells, w_qkv, w_out_t)


def gate_grads(part, count, back, state, state_grad, gain, sig_ref, mix_ref, cell_ref):
    half = state.shape[1] // 2
    low = low_half((count, 2 * half))
    sig, mix, cell = sig_ref[part, :], mix_ref[part, :], cell_ref[part, :]
    arrived = back[part, :].astype(F32)
    new_state = cell + jnp.where(low, arrived, 0.0)
    held = state[part, :].astype(F32)
    given = state_grad[part, :].astype(F32)
    inv_rms = lax.rsqrt(lane_mean(cell * cell, low, half) + EPS)
    scaled = swap_halves(arrived) * jnp.concatenate([gain[...], gain[...]], axis=1)
    along = lane_mean(scaled * cell, low, half)
    hidden = given + inv_rms * scaled - cell * (inv_rms * inv_rms * inv_rms * along)
    hidden = jnp.where(low, hidden, swap_halves(hidden))
    c_new = jnp.where(low, swap_halves(cell), cell)
    c_tanh = jnp.tanh(c_new)
    mix_swapped = swap_halves(mix)
    out_gate = jnp.where(low, mix, mix_swapped)
    given_cell = jnp.where(low, swap_halves(given), given)
    cell_grad = given_cell + hidden * out_gate * (1.0 - c_tanh * c_tanh)
    one = cell_grad * jnp.where(low, mix_swapped, held) * sig * (1.0 - sig)
    two = jnp.where(
        low,
        hidden * c_tanh * mix * (1.0 - mix),
        cell_grad * swap_halves(sig) * (1.0 - mix * mix),
    )
    return one.astype(BF16), two.astype(BF16), cell_grad * sig, new_state


def border_grads(rows, cols):
    def body(*refs):
        out = refs[-1]
        begin = jnp.where(lax.axis_index("gy") == 0, (rows - 1) * cols, 0)
        part = pl.ds(pl.multiple_of(begin, cols), cols)
        one, two, _, _ = gate_grads(part, cols, *refs[:-1])
        out[...] = jnp.concatenate([one, two], axis=1)

    return body


def all_grads(rows, cols, chunk):
    def body(back, state, state_grad, gain, sig_ref, mix_ref, cell_ref,
             new_state, grads, left, right, c_grad):
        count = chunk * cols
        width = state.shape[1]
        for start in range(0, rows, chunk):
            part = pl.ds(start * cols, count)
            one, two, cell, new = gate_grads(
                part, count, back, state, state_grad, gain, sig_ref, mix_ref, cell_ref
            )
            new_state[part, :] = new.astype(BF16)
            c_grad[part, :] = cell.astype(BF16)
            for lanes, value in ((pl.ds(0, width), one), (pl.ds(width, width), two)):
                grads[part, lanes] = value
                left[pl.ds(start, chunk), lanes] = pick_column(value, cols, 0)
                right[pl.ds(start, chunk), lanes] = pick_column(value, cols, cols - 1)

    return body


def step_backward(rows, cols, chunk):
    def body(grads, row_halo, left, right, weights, c_grad, grad_frame, grad_state, taps):
        fill_taps(taps, (grads,), row_halo, left, right, rows, cols, chunk)
        count = chunk * cols
        wide = grad_frame.shape[1]
        for start in range(0, rows, chunk):
            begin = start * cols
            part = pl.ds(begin, count)
            total = conv_backward(taps, weights, begin, count, cols).astype(BF16)
            rest = total.shape[1] - wide
            grad_frame[part, :] = total[:, :wide]
            grad_state[part, pl.ds(0, rest)] = total[:, wide:]
            grad_state[part, pl.ds(rest, rest)] = c_grad[part, pl.ds(rest, rest)]

    return body


def swap_border(first_row, last_row):
    border = jnp.where(lax.axis_index("gy") == 0, last_row, first_row)
    return lax.ppermute(border, "gy", [(0, 1), (1, 0)])


def exchange_columns(first_col, last_col, row_halo):
    count = lax.axis_size("gx")
    forward = [(i, i + 1) for i in range(count - 1)]
    backward = [(target, source) for source, target in forward]
    left = lax.ppermute(jnp.concatenate([last_col, row_halo[-1:]], axis=0), "gx", forward)
    right = lax.ppermute(jnp.concatenate([first_col, row_halo[:1]], axis=0), "gx", backward)
    return row_halo, left, right


def on_device(radar_frame, lstm_state, w_conv, b_gates, norm_gain, w_qkv, w_out, state_grad):
    row_count, col_count, in_channels = radar_frame.shape
    hidden = lstm_state.shape[2] // 2
    gate_dim = w_conv.shape[3]
    attn_dim = w_out.shape[0]
    cells = row_count * col_count
    chunk = min(32, row_count)
    lines = row_count // lax.axis_size("gx")
    shape = lambda *dims: jax.ShapeDtypeStruct(dims, BF16)
    wide = lambda *dims: jax.ShapeDtypeStruct(dims, F32)
    vmem = pltpu.VMEM

    radar = radar_frame.reshape(cells, in_channels)
    state = lstm_state.reshape(cells, 2 * hidden)
    given = state_grad.reshape(cells, 2 * hidden)
    depth = in_channels + 2 * hidden
    both = lambda row: jnp.concatenate([radar_frame[row], lstm_state[row]], axis=-1)
    row_halo = swap_border(both(0), both(-1))
    sems = pltpu.SemaphoreType.DMA
    pieces = row_count // chunk
    in_hbm = lambda array: pltpu.with_memory_space_constraint(array, pltpu.HBM)
    bias, gain = b_gates[None], norm_gain[None]
    left, right, radar, state, bias, gain = call(
        edges(row_count, col_count, chunk),
        (shape(row_count, depth),) * 2
        + (shape(*radar.shape), shape(*state.shape), wide(*bias.shape), wide(*gain.shape)),
        [sems((pieces,)), sems((pieces,)), sems((2,))],
        (0, 1, 2, 3),
        4,
    )(in_hbm(radar), in_hbm(state), in_hbm(bias), in_hbm(gain))
    halo = exchange_columns(left, right, row_halo)

    payload, sig, mix, cell = call(
        step_forward(row_count, col_count, chunk),
        (shape(cells, 2 * hidden),) + (wide(cells, 2 * hidden),) * 3,
        [
            vmem(((row_count + 2) * col_count, 3 * depth), BF16),
            vmem(w_conv.shape, BF16),
            vmem(given.shape, BF16),
            sems((3,)),
            sems((1,)),
        ],
        (5, 8),
        9,
    )(radar, state, *halo, in_hbm(w_conv), bias, gain, in_hbm(given))

    peers = lax.axis_size("gx")
    send = payload.reshape(peers, lines, col_count, 2 * hidden)
    lines_in = lax.all_to_all(send, "gx", split_axis=0, concat_axis=0, tiled=True)
    lines_out = attend(lines_in, w_qkv, w_out.T)
    back = lax.all_to_all(lines_out, "gx", split_axis=0, concat_axis=0, tiled=True)

    back = back.reshape(cells, 2 * hidden)
    operands = (back, state, given, gain, sig, mix, cell)
    border = call(border_grads(row_count, col_count), shape(col_count, gate_dim), count=7)(*operands)
    row_halo = lax.ppermute(border, "gy", [(0, 1), (1, 0)])
    new_state, grads, left, right, c_grad = call(
        all_grads(row_count, col_count, chunk),
        (
            shape(cells, 2 * hidden),
            shape(cells, gate_dim),
            shape(row_count, gate_dim),
            shape(row_count, gate_dim),
            shape(cells, 2 * hidden),
        ),
        count=7,
    )(*operands)
    halo = exchange_columns(left, right, row_halo)
    grad_frame, grad_state = call(
        step_backward(row_count, col_count, chunk),
        (shape(cells, in_channels), shape(cells, 2 * hidden)),
        [vmem(((row_count + 2) * col_count, 3 * gate_dim), BF16)],
        count=6,
    )(grads, *halo, w_conv, c_grad)
    whole = lambda array: array.reshape(row_count, col_count, -1)
    return whole(new_state), whole(grad_frame), whole(grad_state)


def solution(mesh):
    spec = P("gy", "gx", None)
    return jax.shard_map(
        on_device,
        mesh=mesh,
        in_specs=(spec, spec, P(), P(), P(), P(), P(), spec),
        out_specs=(spec, spec, spec),
        check_vma=False,
    )
```

```python
import jax
import jax.numpy as jnp
from jax import lax
from jax.experimental import pallas as pl
from jax.experimental.pallas import tpu as pltpu
from jax.sharding import PartitionSpec as P

HEADS = 8
EPS = 1e-05
LOG2E = 1.4426950408889634
VMEM_ATTEND = 28
F32 = jnp.float32
BF16 = jnp.bfloat16


def matmul(lhs, rhs, lhs_dim=1, rhs_dim=0):
    return lax.dot_general(
        lhs, rhs, (((lhs_dim,), (rhs_dim,)), ((), ())), preferred_element_type=F32
    )


def call(body, out_shape, scratch=(), in_place=(), count=0, vmem=24, cost=None):
    spaces = [pltpu.HBM if index in in_place else pltpu.VMEM for index in range(count)]
    return pl.pallas_call(
        body,
        out_shape=out_shape,
        in_specs=[pl.BlockSpec(memory_space=space) for space in spaces],
        scratch_shapes=list(scratch),
        cost_estimate=cost,
        compiler_params=pltpu.CompilerParams(vmem_limit_bytes=vmem << 20),
    )


def low_half(shape):
    return lax.broadcasted_iota(jnp.int32, shape, 1) < shape[1] // 2


def swap_halves(value):
    return pltpu.roll(value, value.shape[1] // 2, axis=1)


def column_of(shape, cols):
    return lax.rem(lax.broadcasted_iota(jnp.int32, shape, 0), cols)


def spread(edge, cols, at):
    rows = edge.shape[0]
    shape = (rows * cols, rows)
    position = lax.broadcasted_iota(jnp.int32, shape, 0)
    row = lax.broadcasted_iota(jnp.int32, shape, 1)
    pick = jnp.where(position == row * cols + at, 1.0, 0.0).astype(BF16)
    return matmul(pick, edge)


def pick_column(flat, cols, at):
    rows = flat.shape[0] // cols
    shape = (rows, rows * cols)
    row = lax.broadcasted_iota(jnp.int32, shape, 0)
    position = lax.broadcasted_iota(jnp.int32, shape, 1)
    pick = jnp.where(position == row * cols + at, 1.0, 0.0).astype(BF16)
    return matmul(pick, flat).astype(BF16)


def even_place():
    return lax.rem(lax.axis_index("gx"), 2) == 0


def sides(cols):
    even = even_place()
    return jnp.where(even, cols - 1, 0), jnp.where(even, 0, cols - 1)


def fill_taps(taps, parts, row_halo, near, far, rows, cols, chunk):
    even = even_place()
    left = lambda *at: jnp.where(even, far[at].astype(F32), near[at].astype(F32)).astype(BF16)
    right = lambda *at: jnp.where(even, near[at].astype(F32), far[at].astype(F32)).astype(BF16)
    width = taps.shape[1] // 3
    upper = lax.axis_index("gy") == 0
    for start in range(0, rows, chunk):
        count = chunk * cols
        begin = start * cols
        column = 0
        for part in parts:
            part_width = part.shape[1]
            value = part[pl.ds(begin, count), :]
            wide = value.astype(F32)
            where = column_of(wide.shape, cols)
            lanes = pl.ds(column, part_width)
            left_edge = spread(left(pl.ds(start, chunk), lanes), cols, 0)
            right_edge = spread(right(pl.ds(start, chunk), lanes), cols, cols - 1)
            before = jnp.where(where == 0, left_edge, pltpu.roll(wide, 1, axis=0))
            after = jnp.where(where == cols - 1, right_edge, pltpu.roll(wide, count - 1, axis=0))
            target = pl.ds(cols + begin, count)
            taps[target, pl.ds(column, part_width)] = before.astype(BF16)
            taps[target, pl.ds(width + column, part_width)] = value
            taps[target, pl.ds(2 * width + column, part_width)] = after.astype(BF16)
            column += part_width
    halo = row_halo[...].astype(F32)
    where = column_of(halo.shape, cols)
    first = jnp.broadcast_to(left(pl.ds(rows, 1), slice(None)).astype(F32), halo.shape)
    last = jnp.broadcast_to(right(pl.ds(rows, 1), slice(None)).astype(F32), halo.shape)
    before = jnp.where(where == 0, first, pltpu.roll(halo, 1, axis=0))
    after = jnp.where(where == cols - 1, last, pltpu.roll(halo, cols - 1, axis=0))
    for index, piece in enumerate((before, halo, after)):
        lanes = pl.ds(index * width, width)
        taps[pl.ds(0, cols), lanes] = jnp.where(upper, 0.0, piece).astype(BF16)
        taps[pl.ds((rows + 1) * cols, cols), lanes] = jnp.where(upper, piece, 0.0).astype(BF16)


def conv_forward(taps, w_conv, begin, count, cols):
    depth = w_conv.shape[2]
    width = taps.shape[1] // 3
    total = None
    for row_tap in range(3):
        for col_tap in range(3):
            window = taps[pl.ds(begin + row_tap * cols, count), pl.ds(col_tap * width, depth)]
            term = matmul(window, w_conv[row_tap, col_tap])
            total = term if total is None else total + term
    return total


def conv_backward(taps, w_conv, begin, count, cols):
    width = taps.shape[1] // 3
    total = None
    for row_tap in range(3):
        for col_tap in range(3):
            window = taps[pl.ds(begin + row_tap * cols, count), pl.ds(col_tap * width, width)]
            term = matmul(window, w_conv[2 - row_tap, 2 - col_tap], 1, 1)
            total = term if total is None else total + term
    return total


def lane_mean(value, low, size):
    return jnp.sum(jnp.where(low, value, 0.0), axis=-1, keepdims=True) / size


def fetch(source, target, sems, pieces):
    size = source.shape[0] // pieces
    copies = [
        pltpu.make_async_copy(
            source.at[pl.ds(index * size, size)], target.at[pl.ds(index * size, size)], sems.at[index]
        )
        for index in range(pieces)
    ]
    for copy in copies:
        copy.start()
    return copies


def edges(rows, cols, chunk):
    pieces = rows // chunk

    def body(radar, state, bias_in, gain_in, near, far, radar_here, state_here, bias, gain,
             radar_sems, state_sems, sems):
        small = (
            pltpu.make_async_copy(bias_in, bias, sems.at[0]),
            pltpu.make_async_copy(gain_in, gain, sems.at[1]),
        )
        ready = (
            fetch(radar, radar_here, radar_sems, pieces),
            fetch(state, state_here, state_sems, pieces),
        )
        for copy in small:
            copy.start()
        width = radar.shape[1]
        near_at, far_at = sides(cols)
        for index in range(pieces):
            for part, copies, lanes in (
                (radar_here, ready[0], pl.ds(0, width)),
                (state_here, ready[1], pl.ds(width, state.shape[1])),
            ):
                copies[index].wait()
                value = part[pl.ds(index * chunk * cols, chunk * cols), :]
                near[pl.ds(index * chunk, chunk), lanes] = pick_column(value, cols, near_at)
                far[pl.ds(index * chunk, chunk), lanes] = pick_column(value, cols, far_at)
        for copy in small:
            copy.wait()

    return body


def step_forward(rows, cols, chunk):
    def body(radar, state, row_halo, near, far, weights_out, bias, gain, grad_out,
             payload, sig_ref, mix_ref, cell_ref, taps, weights, state_grad, sems, grad_sems):
        later = fetch(weights_out, weights, sems, 3) + fetch(grad_out, state_grad, grad_sems, 1)
        fill_taps(taps, (radar, state), row_halo, near, far, rows, cols, chunk)
        for copy in later:
            copy.wait()
        count = chunk * cols
        half = state.shape[1] // 2
        for start in range(0, rows, chunk):
            begin = start * cols
            part = pl.ds(begin, count)
            gates = conv_forward(taps, weights, begin, count, cols) + bias[...]
            low = low_half((count, 2 * half))
            sig = jax.nn.sigmoid(gates[:, : 2 * half])
            other = gates[:, 2 * half :]
            mix = jnp.where(low, jax.nn.sigmoid(other), jnp.tanh(other))
            held = state[part, :].astype(F32)
            terms = sig * jnp.where(low, swap_halves(mix), held)
            c_new = terms + swap_halves(terms)
            h_new = mix * jnp.tanh(c_new)
            inv_rms = lax.rsqrt(lane_mean(h_new * h_new, low, half) + EPS)
            normed = h_new * inv_rms * jnp.concatenate([gain[...], gain[...]], axis=1)
            grad = swap_halves(state_grad[part, :].astype(F32))
            payload[part, :] = jnp.where(low, normed, grad).astype(BF16)
            sig_ref[part, :] = sig
            mix_ref[part, :] = mix
            cell_ref[part, :] = jnp.where(low, h_new, c_new)

    return body


def attention(length, block, group):
    def body(cells, w_qkv, w_out_t, out, w_qkv_t, rows, cols, mixed, grad_q, grad_k, grad_v,
             *per_head):
        step = pl.program_id(1)
        size = w_out_t.shape[1]
        dim = size // HEADS
        scale = dim ** (-0.5)
        scratches = [per_head[6 * index : 6 * index + 6] for index in range(group)]

        @pl.when(step == 0)
        def _():
            line = cells[...].reshape(length, cells.shape[-1]).astype(F32)
            half = line.shape[1] // 2
            normed = line[:, :half].astype(BF16)
            given = swap_halves(line)[:, :half].astype(BF16)
            w_qkv_t[...] = w_qkv[...].astype(F32).T.astype(BF16)
            w_out = w_out_t[...].astype(F32).T.astype(BF16)
            rows[...] = matmul(normed, w_qkv[:, pl.ds(size, 2 * size)]).astype(BF16)
            cols[pl.ds(0, 3 * size), :] = matmul(w_qkv_t[...], normed, 1, 1).astype(BF16)
            cols[pl.ds(3 * size, size), :] = matmul(w_out, given, 1, 1).astype(BF16)
            for _, _, values, _, _, _ in scratches:
                values[pl.ds(dim, dim), :] = jnp.ones((dim, length), BF16)

        for index, scratch in enumerate(scratches):
            query_mask, grad_mask, values, exps, probs, scores = scratch
            at = pl.multiple_of((step * group + index) * dim, dim)
            mine = pl.ds(at, dim)
            query_cols = cols[mine, :]
            key_cols = cols[pl.ds(size + at, dim), :]
            grad_cols = cols[pl.ds(3 * size + at, dim), :]
            query_mask[...] = jnp.zeros_like(query_mask)
            grad_mask[...] = jnp.zeros_like(grad_mask)
            query_mask[mine, :] = query_cols
            grad_mask[mine, :] = grad_cols
            values[pl.ds(0, dim), :] = cols[pl.ds(2 * size + at, dim), :]
            for begin in range(0, length, block):
                part = pl.ds(begin, block)
                exps[:, part] = jnp.exp2(
                    matmul(rows[:, pl.ds(0, size)], query_mask[:, part]) * (scale * LOG2E)
                ).astype(BF16)
                sums = matmul(values[...], exps[:, part])
                inverse = 1.0 / sums[dim : dim + 1]
                attended = sums[:dim] * inverse
                mixed[mine, part] = attended.astype(BF16)
                grads = cols[pl.ds(3 * size + at, dim), part].astype(F32)
                inner = jnp.sum(attended * grads, axis=0, keepdims=True)
                prob = exps[:, part] * inverse.astype(BF16)
                probs[:, part] = prob
                grad_prob = matmul(rows[:, pl.ds(size, size)], grad_mask[:, part])
                scores[:, part] = prob * (grad_prob - inner).astype(BF16)
                grad_q[mine, part] = (matmul(key_cols, scores[:, part]) * scale).astype(BF16)
            grad_k[mine, :] = (matmul(query_cols, scores[...], 1, 1) * scale).astype(BF16)
            grad_v[mine, :] = matmul(grad_cols, probs[...], 1, 1).astype(BF16)

        @pl.when(step == HEADS // group - 1)
        def _():
            w_out = w_out_t[...].astype(F32).T.astype(BF16)
            back = (
                matmul(grad_q[...], w_qkv_t[pl.ds(0, size), :], 0, 0)
                + matmul(grad_k[...], w_qkv_t[pl.ds(size, size), :], 0, 0)
                + matmul(grad_v[...], w_qkv_t[pl.ds(2 * size, size), :], 0, 0)
            )
            result = jnp.concatenate([matmul(mixed[...], w_out, 0, 0), back], axis=1)
            out[...] = result.astype(BF16).reshape(out.shape)

    return body


def attend(cells, w_qkv, w_out_t):
    peers, lines, cols, width = cells.shape
    length = peers * cols
    size = w_out_t.shape[1]
    block, group = min(512, length), 2
    whole = lambda array: pl.BlockSpec(array.shape, lambda i, j: (0,) * array.ndim)
    line_spec = pl.BlockSpec((peers, None, cols, width), lambda i, j: (0, i, 0, 0))
    tall = pltpu.VMEM((size, length), BF16)
    square = pltpu.VMEM((length, length), BF16)
    return pl.pallas_call(
        attention(length, block, group),
        out_shape=jax.ShapeDtypeStruct(cells.shape, BF16),
        grid=(lines, HEADS // group),
        in_specs=[line_spec, whole(w_qkv), whole(w_out_t)],
        out_specs=line_spec,
        scratch_shapes=[
            pltpu.VMEM(w_qkv.shape[::-1], BF16),
            pltpu.VMEM((length, 2 * size), BF16),
            pltpu.VMEM((4 * size, length), BF16),
            tall,
            tall,
            tall,
            tall,
        ]
        + [
            tall,
            tall,
            pltpu.VMEM((2 * size // HEADS, length), BF16),
            square,
            square,
            square,
        ]
        * group,
        compiler_params=pltpu.CompilerParams(
            dimension_semantics=("arbitrary", "arbitrary"), vmem_limit_bytes=VMEM_ATTEND << 20
        ),
    )(cells, w_qkv, w_out_t)


def gate_grads(part, count, back, state, state_grad, gain, sig_ref, mix_ref, cell_ref):
    half = state.shape[1] // 2
    low = low_half((count, 2 * half))
    sig, mix, cell = sig_ref[part, :], mix_ref[part, :], cell_ref[part, :]
    arrived = back[part, :].astype(F32)
    new_state = cell + jnp.where(low, arrived, 0.0)
    held = state[part, :].astype(F32)
    given = state_grad[part, :].astype(F32)
    inv_rms = lax.rsqrt(lane_mean(cell * cell, low, half) + EPS)
    scaled = swap_halves(arrived) * jnp.concatenate([gain[...], gain[...]], axis=1)
    along = lane_mean(scaled * cell, low, half)
    hidden = given + inv_rms * scaled - cell * (inv_rms * inv_rms * inv_rms * along)
    hidden = jnp.where(low, hidden, swap_halves(hidden))
    c_new = jnp.where(low, swap_halves(cell), cell)
    c_tanh = jnp.tanh(c_new)
    mix_swapped = swap_halves(mix)
    out_gate = jnp.where(low, mix, mix_swapped)
    given_cell = jnp.where(low, swap_halves(given), given)
    cell_grad = given_cell + hidden * out_gate * (1.0 - c_tanh * c_tanh)
    one = cell_grad * jnp.where(low, mix_swapped, held) * sig * (1.0 - sig)
    two = jnp.where(
        low,
        hidden * c_tanh * mix * (1.0 - mix),
        cell_grad * swap_halves(sig) * (1.0 - mix * mix),
    )
    return one.astype(BF16), two.astype(BF16), cell_grad * sig, new_state


def border_grads(rows, cols):
    def body(*refs):
        out = refs[-1]
        begin = jnp.where(lax.axis_index("gy") == 0, (rows - 1) * cols, 0)
        part = pl.ds(pl.multiple_of(begin, cols), cols)
        one, two, _, _ = gate_grads(part, cols, *refs[:-1])
        out[...] = jnp.concatenate([one, two], axis=1)

    return body


def all_grads(rows, cols, chunk):
    def body(back, state, state_grad, gain, sig_ref, mix_ref, cell_ref,
             new_state, grads, near, far, c_grad):
        near_at, far_at = sides(cols)
        count = chunk * cols
        width = state.shape[1]
        for start in range(0, rows, chunk):
            part = pl.ds(start * cols, count)
            one, two, cell, new = gate_grads(
                part, count, back, state, state_grad, gain, sig_ref, mix_ref, cell_ref
            )
            new_state[part, :] = new.astype(BF16)
            c_grad[part, :] = cell.astype(BF16)
            for lanes, value in ((pl.ds(0, width), one), (pl.ds(width, width), two)):
                grads[part, lanes] = value
                near[pl.ds(start, chunk), lanes] = pick_column(value, cols, near_at)
                far[pl.ds(start, chunk), lanes] = pick_column(value, cols, far_at)

    return body


def step_backward(rows, cols, chunk):
    def body(grads, row_halo, near, far, weights, c_grad, grad_frame, grad_state, taps):
        fill_taps(taps, (grads,), row_halo, near, far, rows, cols, chunk)
        count = chunk * cols
        wide = grad_frame.shape[1]
        for start in range(0, rows, chunk):
            begin = start * cols
            part = pl.ds(begin, count)
            total = conv_backward(taps, weights, begin, count, cols).astype(BF16)
            rest = total.shape[1] - wide
            grad_frame[part, :] = total[:, :wide]
            grad_state[part, pl.ds(0, rest)] = total[:, wide:]
            grad_state[part, pl.ds(rest, rest)] = c_grad[part, pl.ds(rest, rest)]

    return body


def swap_border(first_row, last_row):
    border = jnp.where(lax.axis_index("gy") == 0, last_row, first_row)
    return lax.ppermute(border, "gy", [(0, 1), (1, 0)])


def exchange_columns(near, far, row_halo):
    count = lax.axis_size("gx")
    swaps = lambda first: [
        pair for i in range(first, count - 1, 2) for pair in ((i, i + 1), (i + 1, i))
    ]
    even = even_place()
    near_cell = jnp.where(even, row_halo[-1:], row_halo[:1])
    far_cell = jnp.where(even, row_halo[:1], row_halo[-1:])
    near = lax.ppermute(jnp.concatenate([near, near_cell], axis=0), "gx", swaps(0))
    far = lax.ppermute(jnp.concatenate([far, far_cell], axis=0), "gx", swaps(1))
    return row_halo, near, far


def on_device(radar_frame, lstm_state, w_conv, b_gates, norm_gain, w_qkv, w_out, state_grad):
    row_count, col_count, in_channels = radar_frame.shape
    hidden = lstm_state.shape[2] // 2
    gate_dim = w_conv.shape[3]
    attn_dim = w_out.shape[0]
    cells = row_count * col_count
    chunk = min(32, row_count)
    lines = row_count // lax.axis_size("gx")
    shape = lambda *dims: jax.ShapeDtypeStruct(dims, BF16)
    wide = lambda *dims: jax.ShapeDtypeStruct(dims, F32)
    vmem = pltpu.VMEM

    radar = radar_frame.reshape(cells, in_channels)
    state = lstm_state.reshape(cells, 2 * hidden)
    given = state_grad.reshape(cells, 2 * hidden)
    depth = in_channels + 2 * hidden
    both = lambda row: jnp.concatenate([radar_frame[row], lstm_state[row]], axis=-1)
    row_halo = swap_border(both(0), both(-1))
    sems = pltpu.SemaphoreType.DMA
    pieces = row_count // chunk
    in_hbm = lambda array: pltpu.with_memory_space_constraint(array, pltpu.HBM)
    bias, gain = b_gates[None], norm_gain[None]
    near, far, radar, state, bias, gain = call(
        edges(row_count, col_count, chunk),
        (shape(row_count, depth),) * 2
        + (shape(*radar.shape), shape(*state.shape), wide(*bias.shape), wide(*gain.shape)),
        [sems((pieces,)), sems((pieces,)), sems((2,))],
        (0, 1, 2, 3),
        4,
    )(in_hbm(radar), in_hbm(state), in_hbm(bias), in_hbm(gain))
    halo = exchange_columns(near, far, row_halo)

    payload, sig, mix, cell = call(
        step_forward(row_count, col_count, chunk),
        (shape(cells, 2 * hidden),) + (wide(cells, 2 * hidden),) * 3,
        [
            vmem(((row_count + 2) * col_count, 3 * depth), BF16),
            vmem(w_conv.shape, BF16),
            vmem(given.shape, BF16),
            sems((3,)),
            sems((1,)),
        ],
        (5, 8),
        9,
    )(radar, state, *halo, in_hbm(w_conv), bias, gain, in_hbm(given))

    peers = lax.axis_size("gx")
    send = payload.reshape(peers, lines, col_count, 2 * hidden)
    lines_in = lax.all_to_all(send, "gx", split_axis=0, concat_axis=0, tiled=True)
    lines_out = attend(lines_in, w_qkv, w_out.T)
    back = lax.all_to_all(lines_out, "gx", split_axis=0, concat_axis=0, tiled=True)

    back = back.reshape(cells, 2 * hidden)
    operands = (back, state, given, gain, sig, mix, cell)
    border = call(border_grads(row_count, col_count), shape(col_count, gate_dim), count=7)(*operands)
    row_halo = lax.ppermute(border, "gy", [(0, 1), (1, 0)])
    new_state, grads, near, far, c_grad = call(
        all_grads(row_count, col_count, chunk),
        (
            shape(cells, 2 * hidden),
            shape(cells, gate_dim),
            shape(row_count, gate_dim),
            shape(row_count, gate_dim),
            shape(cells, 2 * hidden),
        ),
        count=7,
        cost=pl.CostEstimate(
            flops=64 * cells * gate_dim, transcendentals=4 * cells * hidden, bytes_accessed=24 * cells * gate_dim
        ),
    )(*operands)
    halo = exchange_columns(near, far, row_halo)
    grad_frame, grad_state = call(
        step_backward(row_count, col_count, chunk),
        (shape(cells, in_channels), shape(cells, 2 * hidden)),
        [vmem(((row_count + 2) * col_count, 3 * gate_dim), BF16)],
        count=6,
    )(grads, *halo, w_conv, c_grad)
    whole = lambda array: array.reshape(row_count, col_count, -1)
    return whole(new_state), whole(grad_frame), whole(grad_state)


def solution(mesh):
    spec = P("gy", "gx", None)
    return jax.shard_map(
        on_device,
        mesh=mesh,
        in_specs=(spec, spec, P(), P(), P(), P(), P(), spec),
        out_specs=(spec, spec, spec),
        check_vma=False,
    )
```

```python
import jax
import jax.numpy as jnp
from jax import lax
from jax.experimental import pallas as pl
from jax.experimental.pallas import tpu as pltpu
from jax.sharding import PartitionSpec as P

HEADS = 8
EPS = 1e-05
LOG2E = 1.4426950408889634
VMEM_ATTEND = 36
F32 = jnp.float32
BF16 = jnp.bfloat16


def matmul(lhs, rhs, lhs_dim=1, rhs_dim=0):
    return lax.dot_general(
        lhs, rhs, (((lhs_dim,), (rhs_dim,)), ((), ())), preferred_element_type=F32
    )


def call(body, out_shape, scratch=(), in_place=(), count=0, vmem=24, cost=None):
    spaces = [pltpu.HBM if index in in_place else pltpu.VMEM for index in range(count)]
    return pl.pallas_call(
        body,
        out_shape=out_shape,
        in_specs=[pl.BlockSpec(memory_space=space) for space in spaces],
        scratch_shapes=list(scratch),
        cost_estimate=cost,
        compiler_params=pltpu.CompilerParams(vmem_limit_bytes=vmem << 20),
    )


def low_half(shape):
    return lax.broadcasted_iota(jnp.int32, shape, 1) < shape[1] // 2


def swap_halves(value):
    return pltpu.roll(value, value.shape[1] // 2, axis=1)


def column_of(shape, cols):
    return lax.rem(lax.broadcasted_iota(jnp.int32, shape, 0), cols)


def spread(edge, cols, at):
    rows = edge.shape[0]
    shape = (rows * cols, rows)
    position = lax.broadcasted_iota(jnp.int32, shape, 0)
    row = lax.broadcasted_iota(jnp.int32, shape, 1)
    pick = jnp.where(position == row * cols + at, 1.0, 0.0).astype(BF16)
    return matmul(pick, edge)


def pick_column(flat, cols, at):
    rows = flat.shape[0] // cols
    shape = (rows, rows * cols)
    row = lax.broadcasted_iota(jnp.int32, shape, 0)
    position = lax.broadcasted_iota(jnp.int32, shape, 1)
    pick = jnp.where(position == row * cols + at, 1.0, 0.0).astype(BF16)
    return matmul(pick, flat).astype(BF16)


def even_place():
    return lax.rem(lax.axis_index("gx"), 2) == 0


def sides(cols):
    even = even_place()
    return jnp.where(even, cols - 1, 0), jnp.where(even, 0, cols - 1)


def fill_taps(taps, parts, row_halo, near, far, rows, cols, chunk):
    even = even_place()
    left = lambda *at: jnp.where(even, far[at].astype(F32), near[at].astype(F32)).astype(BF16)
    right = lambda *at: jnp.where(even, near[at].astype(F32), far[at].astype(F32)).astype(BF16)
    width = taps.shape[1] // 3
    upper = lax.axis_index("gy") == 0
    for start in range(0, rows, chunk):
        count = chunk * cols
        begin = start * cols
        column = 0
        for part in parts:
            part_width = part.shape[1]
            value = part[pl.ds(begin, count), :]
            wide = value.astype(F32)
            where = column_of(wide.shape, cols)
            lanes = pl.ds(column, part_width)
            left_edge = spread(left(pl.ds(start, chunk), lanes), cols, 0)
            right_edge = spread(right(pl.ds(start, chunk), lanes), cols, cols - 1)
            before = jnp.where(where == 0, left_edge, pltpu.roll(wide, 1, axis=0))
            after = jnp.where(where == cols - 1, right_edge, pltpu.roll(wide, count - 1, axis=0))
            target = pl.ds(cols + begin, count)
            taps[target, pl.ds(column, part_width)] = before.astype(BF16)
            taps[target, pl.ds(width + column, part_width)] = value
            taps[target, pl.ds(2 * width + column, part_width)] = after.astype(BF16)
            column += part_width
    halo = row_halo[...].astype(F32)
    where = column_of(halo.shape, cols)
    first = jnp.broadcast_to(left(pl.ds(rows, 1), slice(None)).astype(F32), halo.shape)
    last = jnp.broadcast_to(right(pl.ds(rows, 1), slice(None)).astype(F32), halo.shape)
    before = jnp.where(where == 0, first, pltpu.roll(halo, 1, axis=0))
    after = jnp.where(where == cols - 1, last, pltpu.roll(halo, cols - 1, axis=0))
    for index, piece in enumerate((before, halo, after)):
        lanes = pl.ds(index * width, width)
        taps[pl.ds(0, cols), lanes] = jnp.where(upper, 0.0, piece).astype(BF16)
        taps[pl.ds((rows + 1) * cols, cols), lanes] = jnp.where(upper, piece, 0.0).astype(BF16)


def conv_forward(taps, w_conv, begin, count, cols):
    depth = w_conv.shape[2]
    width = taps.shape[1] // 3
    total = None
    for row_tap in range(3):
        for col_tap in range(3):
            window = taps[pl.ds(begin + row_tap * cols, count), pl.ds(col_tap * width, depth)]
            term = matmul(window, w_conv[row_tap, col_tap])
            total = term if total is None else total + term
    return total


def conv_backward(taps, w_conv, begin, count, cols):
    width = taps.shape[1] // 3
    total = None
    for row_tap in range(3):
        for col_tap in range(3):
            window = taps[pl.ds(begin + row_tap * cols, count), pl.ds(col_tap * width, width)]
            term = matmul(window, w_conv[2 - row_tap, 2 - col_tap], 1, 1)
            total = term if total is None else total + term
    return total


def lane_mean(value, low, size):
    return jnp.sum(jnp.where(low, value, 0.0), axis=-1, keepdims=True) / size


def fetch(source, target, sems, pieces):
    size = source.shape[0] // pieces
    copies = [
        pltpu.make_async_copy(
            source.at[pl.ds(index * size, size)], target.at[pl.ds(index * size, size)], sems.at[index]
        )
        for index in range(pieces)
    ]
    for copy in copies:
        copy.start()
    return copies


def edges(rows, cols, chunk):
    pieces = rows // chunk

    def body(radar, state, bias_in, gain_in, near, far, radar_here, state_here, bias, gain,
             radar_sems, state_sems, sems):
        small = (
            pltpu.make_async_copy(bias_in, bias, sems.at[0]),
            pltpu.make_async_copy(gain_in, gain, sems.at[1]),
        )
        ready = (
            fetch(radar, radar_here, radar_sems, pieces),
            fetch(state, state_here, state_sems, pieces),
        )
        for copy in small:
            copy.start()
        width = radar.shape[1]
        near_at, far_at = sides(cols)
        for index in range(pieces):
            for part, copies, lanes in (
                (radar_here, ready[0], pl.ds(0, width)),
                (state_here, ready[1], pl.ds(width, state.shape[1])),
            ):
                copies[index].wait()
                value = part[pl.ds(index * chunk * cols, chunk * cols), :]
                near[pl.ds(index * chunk, chunk), lanes] = pick_column(value, cols, near_at)
                far[pl.ds(index * chunk, chunk), lanes] = pick_column(value, cols, far_at)
        for copy in small:
            copy.wait()

    return body


def step_forward(rows, cols, chunk):
    def body(radar, state, row_halo, near, far, weights, bias, gain, state_grad,
             payload, sig_ref, mix_ref, cell_ref, taps):
        fill_taps(taps, (radar, state), row_halo, near, far, rows, cols, chunk)
        count = chunk * cols
        half = state.shape[1] // 2
        for start in range(0, rows, chunk):
            begin = start * cols
            part = pl.ds(begin, count)
            gates = conv_forward(taps, weights, begin, count, cols) + bias[...]
            low = low_half((count, 2 * half))
            sig = jax.nn.sigmoid(gates[:, : 2 * half])
            other = gates[:, 2 * half :]
            mix = jnp.where(low, jax.nn.sigmoid(other), jnp.tanh(other))
            held = state[part, :].astype(F32)
            terms = sig * jnp.where(low, swap_halves(mix), held)
            c_new = terms + swap_halves(terms)
            h_new = mix * jnp.tanh(c_new)
            inv_rms = lax.rsqrt(lane_mean(h_new * h_new, low, half) + EPS)
            normed = h_new * inv_rms * jnp.concatenate([gain[...], gain[...]], axis=1)
            grad = swap_halves(state_grad[part, :].astype(F32))
            payload[part, :] = jnp.where(low, normed, grad).astype(BF16)
            sig_ref[part, :] = sig
            mix_ref[part, :] = mix
            cell_ref[part, :] = jnp.where(low, h_new, c_new)

    return body


def attention(length, block, group):
    def body(cells, w_qkv, w_out_t, out, w_qkv_t, rows, cols, mixed, grad_q, grad_k, grad_v,
             *per_head):
        size = w_out_t.shape[1]
        dim = size // HEADS
        scale = dim ** (-0.5)
        scratches = [per_head[6 * index : 6 * index + 6] for index in range(group)]
        w_qkv_t[...] = w_qkv[...].astype(F32).T.astype(BF16)
        for query_mask, grad_mask, values, _, _, _ in scratches:
            query_mask[...] = jnp.zeros_like(query_mask)
            grad_mask[...] = jnp.zeros_like(grad_mask)
            values[pl.ds(dim, dim), :] = jnp.ones((dim, length), BF16)

        def one_head(head, query_mask, grad_mask, values, exps, probs, scores):
            at = pl.multiple_of(head * dim, dim)
            mine = pl.ds(at, dim)
            query_cols = cols[mine, :]
            key_cols = cols[pl.ds(size + at, dim), :]
            grad_cols = cols[pl.ds(3 * size + at, dim), :]
            query_mask[mine, :] = query_cols
            grad_mask[mine, :] = grad_cols
            values[pl.ds(0, dim), :] = cols[pl.ds(2 * size + at, dim), :]
            for begin in range(0, length, block):
                part = pl.ds(begin, block)
                exps[:, part] = jnp.exp2(
                    matmul(rows[:, pl.ds(0, size)], query_mask[:, part]) * (scale * LOG2E)
                ).astype(BF16)
                sums = matmul(values[...], exps[:, part])
                inverse = 1.0 / sums[dim : dim + 1]
                attended = sums[:dim] * inverse
                mixed[mine, part] = attended.astype(BF16)
                grads = cols[pl.ds(3 * size + at, dim), part].astype(F32)
                inner = jnp.sum(attended * grads, axis=0, keepdims=True)
                prob = exps[:, part] * inverse.astype(BF16)
                probs[:, part] = prob
                grad_prob = matmul(rows[:, pl.ds(size, size)], grad_mask[:, part])
                scores[:, part] = prob * (grad_prob - inner).astype(BF16)
                grad_q[mine, part] = (matmul(key_cols, scores[:, part]) * scale).astype(BF16)
            grad_k[mine, :] = (matmul(query_cols, scores[...], 1, 1) * scale).astype(BF16)
            grad_v[mine, :] = matmul(grad_cols, probs[...], 1, 1).astype(BF16)
            query_mask[mine, :] = jnp.zeros_like(query_cols)
            grad_mask[mine, :] = jnp.zeros_like(grad_cols)

        def heads(step, carry):
            for index, scratch in enumerate(scratches):
                one_head(step * group + index, *scratch)
            return carry

        def row(index, carry):
            here = (slice(None), pl.ds(index, 1))
            line = cells[here].reshape(length, cells.shape[-1]).astype(F32)
            half = line.shape[1] // 2
            normed = line[:, :half].astype(BF16)
            given = swap_halves(line)[:, :half].astype(BF16)
            w_out = w_out_t[...].astype(F32).T.astype(BF16)
            rows[...] = matmul(normed, w_qkv[:, pl.ds(size, 2 * size)]).astype(BF16)
            cols[pl.ds(0, 3 * size), :] = matmul(w_qkv_t[...], normed, 1, 1).astype(BF16)
            cols[pl.ds(3 * size, size), :] = matmul(w_out, given, 1, 1).astype(BF16)
            lax.fori_loop(0, HEADS // group, heads, 0)
            back = (
                matmul(grad_q[...], w_qkv_t[pl.ds(0, size), :], 0, 0)
                + matmul(grad_k[...], w_qkv_t[pl.ds(size, size), :], 0, 0)
                + matmul(grad_v[...], w_qkv_t[pl.ds(2 * size, size), :], 0, 0)
            )
            result = jnp.concatenate([matmul(mixed[...], w_out, 0, 0), back], axis=1)
            peers, _, cells_each, width = cells.shape
            out[here] = result.astype(BF16).reshape(peers, 1, cells_each, width)
            return carry

        lax.fori_loop(0, cells.shape[1], row, 0)

    return body


def attend(cells, w_qkv, w_out_t):
    peers, lines, cols, width = cells.shape
    length = peers * cols
    size = w_out_t.shape[1]
    block, group = min(512, length), 4
    tall = pltpu.VMEM((size, length), BF16)
    square = pltpu.VMEM((length, length), BF16)
    return call(
        attention(length, block, group),
        jax.ShapeDtypeStruct(cells.shape, BF16),
        [
            pltpu.VMEM(w_qkv.shape[::-1], BF16),
            pltpu.VMEM((length, 2 * size), BF16),
            pltpu.VMEM((4 * size, length), BF16),
            tall,
            tall,
            tall,
            tall,
        ]
        + [
            tall,
            tall,
            pltpu.VMEM((2 * size // HEADS, length), BF16),
            square,
            square,
            square,
        ]
        * group,
        count=3,
        vmem=VMEM_ATTEND,
    )(cells, w_qkv, w_out_t)


def gate_grads(part, count, back, state, state_grad, gain, sig_ref, mix_ref, cell_ref):
    half = state.shape[1] // 2
    low = low_half((count, 2 * half))
    sig, mix, cell = sig_ref[part, :], mix_ref[part, :], cell_ref[part, :]
    arrived = back[part, :].astype(F32)
    new_state = cell + jnp.where(low, arrived, 0.0)
    held = state[part, :].astype(F32)
    given = state_grad[part, :].astype(F32)
    inv_rms = lax.rsqrt(lane_mean(cell * cell, low, half) + EPS)
    scaled = swap_halves(arrived) * jnp.concatenate([gain[...], gain[...]], axis=1)
    along = lane_mean(scaled * cell, low, half)
    hidden = given + inv_rms * scaled - cell * (inv_rms * inv_rms * inv_rms * along)
    hidden = jnp.where(low, hidden, swap_halves(hidden))
    c_new = jnp.where(low, swap_halves(cell), cell)
    c_tanh = jnp.tanh(c_new)
    mix_swapped = swap_halves(mix)
    out_gate = jnp.where(low, mix, mix_swapped)
    given_cell = jnp.where(low, swap_halves(given), given)
    cell_grad = given_cell + hidden * out_gate * (1.0 - c_tanh * c_tanh)
    one = cell_grad * jnp.where(low, mix_swapped, held) * sig * (1.0 - sig)
    two = jnp.where(
        low,
        hidden * c_tanh * mix * (1.0 - mix),
        cell_grad * swap_halves(sig) * (1.0 - mix * mix),
    )
    return one.astype(BF16), two.astype(BF16), cell_grad * sig, new_state


def border_grads(rows, cols):
    def body(*refs):
        out = refs[-1]
        begin = jnp.where(lax.axis_index("gy") == 0, (rows - 1) * cols, 0)
        part = pl.ds(pl.multiple_of(begin, cols), cols)
        one, two, _, _ = gate_grads(part, cols, *refs[:-1])
        out[...] = jnp.concatenate([one, two], axis=1)

    return body


def all_grads(rows, cols, chunk):
    def body(back, state, state_grad, gain, sig_ref, mix_ref, cell_ref,
             new_state, grads, near, far, c_grad):
        near_at, far_at = sides(cols)
        count = chunk * cols
        width = state.shape[1]
        for start in range(0, rows, chunk):
            part = pl.ds(start * cols, count)
            one, two, cell, new = gate_grads(
                part, count, back, state, state_grad, gain, sig_ref, mix_ref, cell_ref
            )
            new_state[part, :] = new.astype(BF16)
            c_grad[part, :] = cell.astype(BF16)
            for lanes, value in ((pl.ds(0, width), one), (pl.ds(width, width), two)):
                grads[part, lanes] = value
                near[pl.ds(start, chunk), lanes] = pick_column(value, cols, near_at)
                far[pl.ds(start, chunk), lanes] = pick_column(value, cols, far_at)

    return body


def step_backward(rows, cols, chunk):
    def body(grads, row_halo, near, far, weights, c_grad, grad_frame, grad_state, taps):
        fill_taps(taps, (grads,), row_halo, near, far, rows, cols, chunk)
        count = chunk * cols
        wide = grad_frame.shape[1]
        for start in range(0, rows, chunk):
            begin = start * cols
            part = pl.ds(begin, count)
            total = conv_backward(taps, weights, begin, count, cols).astype(BF16)
            rest = total.shape[1] - wide
            grad_frame[part, :] = total[:, :wide]
            grad_state[part, pl.ds(0, rest)] = total[:, wide:]
            grad_state[part, pl.ds(rest, rest)] = c_grad[part, pl.ds(rest, rest)]

    return body


def swap_border(first_row, last_row):
    border = jnp.where(lax.axis_index("gy") == 0, last_row, first_row)
    return lax.ppermute(border, "gy", [(0, 1), (1, 0)])


def exchange_columns(near, far, row_halo):
    count = lax.axis_size("gx")
    swaps = lambda first: [
        pair for i in range(first, count - 1, 2) for pair in ((i, i + 1), (i + 1, i))
    ]
    even = even_place()
    near_cell = jnp.where(even, row_halo[-1:], row_halo[:1])
    far_cell = jnp.where(even, row_halo[:1], row_halo[-1:])
    near = lax.ppermute(jnp.concatenate([near, near_cell], axis=0), "gx", swaps(0))
    far = lax.ppermute(jnp.concatenate([far, far_cell], axis=0), "gx", swaps(1))
    return row_halo, near, far


def on_device(radar_frame, lstm_state, w_conv, b_gates, norm_gain, w_qkv, w_out, state_grad):
    row_count, col_count, in_channels = radar_frame.shape
    hidden = lstm_state.shape[2] // 2
    gate_dim = w_conv.shape[3]
    attn_dim = w_out.shape[0]
    cells = row_count * col_count
    chunk, long_chunk = min(16, row_count), min(64, row_count)
    lines = row_count // lax.axis_size("gx")
    shape = lambda *dims: jax.ShapeDtypeStruct(dims, BF16)
    wide = lambda *dims: jax.ShapeDtypeStruct(dims, F32)
    vmem = pltpu.VMEM

    radar = radar_frame.reshape(cells, in_channels)
    state = lstm_state.reshape(cells, 2 * hidden)
    given = state_grad.reshape(cells, 2 * hidden)
    depth = in_channels + 2 * hidden
    both = lambda row: jnp.concatenate([radar_frame[row], lstm_state[row]], axis=-1)
    row_halo = swap_border(both(0), both(-1))
    sems = pltpu.SemaphoreType.DMA
    pieces = row_count // long_chunk
    in_hbm = lambda array: pltpu.with_memory_space_constraint(array, pltpu.HBM)
    bias, gain = b_gates[None], norm_gain[None]
    near, far, radar, state, bias, gain = call(
        edges(row_count, col_count, long_chunk),
        (shape(row_count, depth),) * 2
        + (shape(*radar.shape), shape(*state.shape), wide(*bias.shape), wide(*gain.shape)),
        [sems((pieces,)), sems((pieces,)), sems((2,))],
        (0, 1, 2, 3),
        4,
    )(in_hbm(radar), in_hbm(state), in_hbm(bias), in_hbm(gain))
    halo = exchange_columns(near, far, row_halo)

    payload, sig, mix, cell = call(
        step_forward(row_count, col_count, chunk),
        (shape(cells, 2 * hidden),) + (wide(cells, 2 * hidden),) * 3,
        [vmem(((row_count + 2) * col_count, 3 * depth), BF16)],
        count=9,
    )(radar, state, *halo, w_conv, bias, gain, given)

    peers = lax.axis_size("gx")
    send = payload.reshape(peers, lines, col_count, 2 * hidden)
    lines_in = lax.all_to_all(send, "gx", split_axis=0, concat_axis=0, tiled=True)
    lines_out = attend(lines_in, w_qkv, w_out.T)
    back = lax.all_to_all(lines_out, "gx", split_axis=0, concat_axis=0, tiled=True)

    back = back.reshape(cells, 2 * hidden)
    operands = (back, state, given, gain, sig, mix, cell)
    border = call(border_grads(row_count, col_count), shape(col_count, gate_dim), count=7)(*operands)
    row_halo = lax.ppermute(border, "gy", [(0, 1), (1, 0)])
    new_state, grads, near, far, c_grad = call(
        all_grads(row_count, col_count, long_chunk),
        (
            shape(cells, 2 * hidden),
            shape(cells, gate_dim),
            shape(row_count, gate_dim),
            shape(row_count, gate_dim),
            shape(cells, 2 * hidden),
        ),
        count=7,
        cost=pl.CostEstimate(
            flops=64 * cells * gate_dim, transcendentals=4 * cells * hidden, bytes_accessed=24 * cells * gate_dim
        ),
    )(*operands)
    halo = exchange_columns(near, far, row_halo)
    grad_frame, grad_state = call(
        step_backward(row_count, col_count, chunk),
        (shape(cells, in_channels), shape(cells, 2 * hidden)),
        [vmem(((row_count + 2) * col_count, 3 * gate_dim), BF16)],
        count=6,
    )(grads, *halo, w_conv, c_grad)
    whole = lambda array: array.reshape(row_count, col_count, -1)
    return whole(new_state), whole(grad_frame), whole(grad_state)


def solution(mesh):
    spec = P("gy", "gx", None)
    return jax.shard_map(
        on_device,
        mesh=mesh,
        in_specs=(spec, spec, P(), P(), P(), P(), P(), spec),
        out_specs=(spec, spec, spec),
        check_vma=False,
    )
```

```python
import jax
import jax.numpy as jnp
from jax import lax
from jax.experimental import pallas as pl
from jax.experimental.pallas import tpu as pltpu
from jax.sharding import PartitionSpec as P

HEADS = 8
EPS = 1e-05
LOG2E = 1.4426950408889634
VMEM_ATTEND = 36
F32 = jnp.float32
BF16 = jnp.bfloat16


def matmul(lhs, rhs, lhs_dim=1, rhs_dim=0):
    return lax.dot_general(
        lhs, rhs, (((lhs_dim,), (rhs_dim,)), ((), ())), preferred_element_type=F32
    )


def call(body, out_shape, scratch=(), in_place=(), count=0, vmem=24, cost=None,
         sent=()):
    spaces = [pltpu.HBM if index in in_place else pltpu.VMEM for index in range(count)]
    out_specs = None
    if sent:
        out_specs = [
            pl.BlockSpec(memory_space=pl.ANY if index in sent else pltpu.VMEM)
            for index in range(len(out_shape))
        ]
    more = {} if out_specs is None else {"out_specs": tuple(out_specs)}
    return pl.pallas_call(
        body,
        out_shape=out_shape,
        in_specs=[pl.BlockSpec(memory_space=space) for space in spaces],
        scratch_shapes=list(scratch),
        cost_estimate=cost,
        **more,
        compiler_params=pltpu.CompilerParams(vmem_limit_bytes=vmem << 20),
    )


def low_half(shape):
    return lax.broadcasted_iota(jnp.int32, shape, 1) < shape[1] // 2


def swap_halves(value):
    return pltpu.roll(value, value.shape[1] // 2, axis=1)


def column_of(shape, cols):
    return lax.rem(lax.broadcasted_iota(jnp.int32, shape, 0), cols)


def spread(edge, cols, at):
    rows = edge.shape[0]
    shape = (rows * cols, rows)
    position = lax.broadcasted_iota(jnp.int32, shape, 0)
    row = lax.broadcasted_iota(jnp.int32, shape, 1)
    pick = jnp.where(position == row * cols + at, 1.0, 0.0).astype(BF16)
    return matmul(pick, edge)


def pick_column(flat, cols, at):
    rows = flat.shape[0] // cols
    shape = (rows, rows * cols)
    row = lax.broadcasted_iota(jnp.int32, shape, 0)
    position = lax.broadcasted_iota(jnp.int32, shape, 1)
    pick = jnp.where(position == row * cols + at, 1.0, 0.0).astype(BF16)
    return matmul(pick, flat).astype(BF16)


def even_place():
    return lax.rem(lax.axis_index("gx"), 2) == 0


def sides(cols):
    even = even_place()
    return jnp.where(even, cols - 1, 0), jnp.where(even, 0, cols - 1)


def fill_taps(taps, parts, row_halo, near, far, rows, cols, chunk):
    even = even_place()
    left = lambda *at: jnp.where(even, far[at].astype(F32), near[at].astype(F32)).astype(BF16)
    right = lambda *at: jnp.where(even, near[at].astype(F32), far[at].astype(F32)).astype(BF16)
    width = taps.shape[1] // 3
    upper = lax.axis_index("gy") == 0
    for start in range(0, rows, chunk):
        count = chunk * cols
        begin = start * cols
        column = 0
        for part in parts:
            part_width = part.shape[1]
            value = part[pl.ds(begin, count), :]
            wide = value.astype(F32)
            where = column_of(wide.shape, cols)
            lanes = pl.ds(column, part_width)
            left_edge = spread(left(pl.ds(start, chunk), lanes), cols, 0)
            right_edge = spread(right(pl.ds(start, chunk), lanes), cols, cols - 1)
            before = jnp.where(where == 0, left_edge, pltpu.roll(wide, 1, axis=0))
            after = jnp.where(where == cols - 1, right_edge, pltpu.roll(wide, count - 1, axis=0))
            target = pl.ds(cols + begin, count)
            taps[target, pl.ds(column, part_width)] = before.astype(BF16)
            taps[target, pl.ds(width + column, part_width)] = value
            taps[target, pl.ds(2 * width + column, part_width)] = after.astype(BF16)
            column += part_width
    halo = row_halo[...].astype(F32)
    where = column_of(halo.shape, cols)
    first = jnp.broadcast_to(left(pl.ds(rows, 1), slice(None)).astype(F32), halo.shape)
    last = jnp.broadcast_to(right(pl.ds(rows, 1), slice(None)).astype(F32), halo.shape)
    before = jnp.where(where == 0, first, pltpu.roll(halo, 1, axis=0))
    after = jnp.where(where == cols - 1, last, pltpu.roll(halo, cols - 1, axis=0))
    for index, piece in enumerate((before, halo, after)):
        lanes = pl.ds(index * width, width)
        taps[pl.ds(0, cols), lanes] = jnp.where(upper, 0.0, piece).astype(BF16)
        taps[pl.ds((rows + 1) * cols, cols), lanes] = jnp.where(upper, piece, 0.0).astype(BF16)


def conv_forward(taps, w_conv, begin, count, cols):
    depth = w_conv.shape[2]
    width = taps.shape[1] // 3
    total = None
    for row_tap in range(3):
        for col_tap in range(3):
            window = taps[pl.ds(begin + row_tap * cols, count), pl.ds(col_tap * width, depth)]
            term = matmul(window, w_conv[row_tap, col_tap])
            total = term if total is None else total + term
    return total


def conv_backward(taps, w_conv, begin, count, cols):
    width = taps.shape[1] // 3
    total = None
    for row_tap in range(3):
        for col_tap in range(3):
            window = taps[pl.ds(begin + row_tap * cols, count), pl.ds(col_tap * width, width)]
            term = matmul(window, w_conv[2 - row_tap, 2 - col_tap], 1, 1)
            total = term if total is None else total + term
    return total


def lane_mean(value, low, size):
    return jnp.sum(jnp.where(low, value, 0.0), axis=-1, keepdims=True) / size


def fetch(source, target, sems, pieces):
    size = source.shape[0] // pieces
    copies = [
        pltpu.make_async_copy(
            source.at[pl.ds(index * size, size)], target.at[pl.ds(index * size, size)], sems.at[index]
        )
        for index in range(pieces)
    ]
    for copy in copies:
        copy.start()
    return copies


def edges(rows, cols, chunk):
    pieces = rows // chunk

    def body(radar, state, bias_in, gain_in, near, far, radar_here, state_here, bias, gain,
             radar_sems, state_sems, sems):
        small = (
            pltpu.make_async_copy(bias_in, bias, sems.at[0]),
            pltpu.make_async_copy(gain_in, gain, sems.at[1]),
        )
        ready = (
            fetch(radar, radar_here, radar_sems, pieces),
            fetch(state, state_here, state_sems, pieces),
        )
        for copy in small:
            copy.start()
        width = radar.shape[1]
        near_at, far_at = sides(cols)
        for index in range(pieces):
            for part, copies, lanes in (
                (radar_here, ready[0], pl.ds(0, width)),
                (state_here, ready[1], pl.ds(width, state.shape[1])),
            ):
                copies[index].wait()
                value = part[pl.ds(index * chunk * cols, chunk * cols), :]
                near[pl.ds(index * chunk, chunk), lanes] = pick_column(value, cols, near_at)
                far[pl.ds(index * chunk, chunk), lanes] = pick_column(value, cols, far_at)
        for copy in small:
            copy.wait()

    return body


def step_forward(rows, cols, chunk):
    def body(radar, state, row_halo, near, far, weights, bias, gain, state_grad,
             payload, sig_ref, mix_ref, cell_ref, taps):
        fill_taps(taps, (radar, state), row_halo, near, far, rows, cols, chunk)
        count = chunk * cols
        half = state.shape[1] // 2
        for start in range(0, rows, chunk):
            begin = start * cols
            part = pl.ds(begin, count)
            gates = conv_forward(taps, weights, begin, count, cols) + bias[...]
            low = low_half((count, 2 * half))
            sig = jax.nn.sigmoid(gates[:, : 2 * half])
            other = gates[:, 2 * half :]
            mix = jnp.where(low, jax.nn.sigmoid(other), jnp.tanh(other))
            held = state[part, :].astype(F32)
            terms = sig * jnp.where(low, swap_halves(mix), held)
            c_new = terms + swap_halves(terms)
            h_new = mix * jnp.tanh(c_new)
            inv_rms = lax.rsqrt(lane_mean(h_new * h_new, low, half) + EPS)
            normed = h_new * inv_rms * jnp.concatenate([gain[...], gain[...]], axis=1)
            grad = swap_halves(state_grad[part, :].astype(F32))
            payload[part, :] = jnp.where(low, normed, grad).astype(BF16)
            sig_ref[part, :] = sig
            mix_ref[part, :] = mix
            cell_ref[part, :] = jnp.where(low, h_new, c_new)

    return body


def attention(length, block, group):
    def body(cells, w_qkv, w_out_t, out, w_qkv_t, rows, cols, mixed, grad_q, grad_k, grad_v,
             *per_head):
        size = w_out_t.shape[1]
        dim = size // HEADS
        scale = dim ** (-0.5)
        scratches = [per_head[6 * index : 6 * index + 6] for index in range(group)]
        w_qkv_t[...] = w_qkv[...].astype(F32).T.astype(BF16)
        for query_mask, grad_mask, values, _, _, _ in scratches:
            query_mask[...] = jnp.zeros_like(query_mask)
            grad_mask[...] = jnp.zeros_like(grad_mask)
            values[pl.ds(dim, dim), :] = jnp.ones((dim, length), BF16)

        def one_head(head, query_mask, grad_mask, values, exps, probs, scores):
            at = pl.multiple_of(head * dim, dim)
            mine = pl.ds(at, dim)
            query_cols = cols[mine, :]
            key_cols = cols[pl.ds(size + at, dim), :]
            grad_cols = cols[pl.ds(3 * size + at, dim), :]
            query_mask[mine, :] = query_cols
            grad_mask[mine, :] = grad_cols
            values[pl.ds(0, dim), :] = cols[pl.ds(2 * size + at, dim), :]
            for begin in range(0, length, block):
                part = pl.ds(begin, block)
                exps[:, part] = jnp.exp2(
                    matmul(rows[:, pl.ds(0, size)], query_mask[:, part]) * (scale * LOG2E)
                ).astype(BF16)
                sums = matmul(values[...], exps[:, part])
                inverse = 1.0 / sums[dim : dim + 1]
                attended = sums[:dim] * inverse
                mixed[mine, part] = attended.astype(BF16)
                grads = cols[pl.ds(3 * size + at, dim), part].astype(F32)
                inner = jnp.sum(attended * grads, axis=0, keepdims=True)
                prob = exps[:, part] * inverse.astype(BF16)
                probs[:, part] = prob
                grad_prob = matmul(rows[:, pl.ds(size, size)], grad_mask[:, part])
                scores[:, part] = prob * (grad_prob - inner).astype(BF16)
                grad_q[mine, part] = (matmul(key_cols, scores[:, part]) * scale).astype(BF16)
            grad_k[mine, :] = (matmul(query_cols, scores[...], 1, 1) * scale).astype(BF16)
            grad_v[mine, :] = matmul(grad_cols, probs[...], 1, 1).astype(BF16)
            query_mask[mine, :] = jnp.zeros_like(query_cols)
            grad_mask[mine, :] = jnp.zeros_like(grad_cols)

        def heads(step, carry):
            for index, scratch in enumerate(scratches):
                one_head(step * group + index, *scratch)
            return carry

        def row(index, carry):
            here = (slice(None), pl.ds(index, 1))
            line = cells[here].reshape(length, cells.shape[-1]).astype(F32)
            half = line.shape[1] // 2
            normed = line[:, :half].astype(BF16)
            given = swap_halves(line)[:, :half].astype(BF16)
            w_out = w_out_t[...].astype(F32).T.astype(BF16)
            rows[...] = matmul(normed, w_qkv[:, pl.ds(size, 2 * size)]).astype(BF16)
            cols[pl.ds(0, 3 * size), :] = matmul(w_qkv_t[...], normed, 1, 1).astype(BF16)
            cols[pl.ds(3 * size, size), :] = matmul(w_out, given, 1, 1).astype(BF16)
            lax.fori_loop(0, HEADS // group, heads, 0)
            back = (
                matmul(grad_q[...], w_qkv_t[pl.ds(0, size), :], 0, 0)
                + matmul(grad_k[...], w_qkv_t[pl.ds(size, size), :], 0, 0)
                + matmul(grad_v[...], w_qkv_t[pl.ds(2 * size, size), :], 0, 0)
            )
            result = jnp.concatenate([matmul(mixed[...], w_out, 0, 0), back], axis=1)
            peers, _, cells_each, width = cells.shape
            out[here] = result.astype(BF16).reshape(peers, 1, cells_each, width)
            return carry

        lax.fori_loop(0, cells.shape[1], row, 0)

    return body


def attend(cells, w_qkv, w_out_t):
    peers, lines, cols, width = cells.shape
    length = peers * cols
    size = w_out_t.shape[1]
    block, group = min(512, length), 4
    tall = pltpu.VMEM((size, length), BF16)
    square = pltpu.VMEM((length, length), BF16)
    return call(
        attention(length, block, group),
        jax.ShapeDtypeStruct(cells.shape, BF16),
        [
            pltpu.VMEM(w_qkv.shape[::-1], BF16),
            pltpu.VMEM((length, 2 * size), BF16),
            pltpu.VMEM((4 * size, length), BF16),
            tall,
            tall,
            tall,
            tall,
        ]
        + [
            tall,
            tall,
            pltpu.VMEM((2 * size // HEADS, length), BF16),
            square,
            square,
            square,
        ]
        * group,
        count=3,
        vmem=VMEM_ATTEND,
    )(cells, w_qkv, w_out_t)


def gate_grads(part, count, back, state, state_grad, gain, sig_ref, mix_ref, cell_ref):
    half = state.shape[1] // 2
    low = low_half((count, 2 * half))
    sig, mix, cell = sig_ref[part, :], mix_ref[part, :], cell_ref[part, :]
    arrived = back[part, :].astype(F32)
    new_state = cell + jnp.where(low, arrived, 0.0)
    held = state[part, :].astype(F32)
    given = state_grad[part, :].astype(F32)
    inv_rms = lax.rsqrt(lane_mean(cell * cell, low, half) + EPS)
    scaled = swap_halves(arrived) * jnp.concatenate([gain[...], gain[...]], axis=1)
    along = lane_mean(scaled * cell, low, half)
    hidden = given + inv_rms * scaled - cell * (inv_rms * inv_rms * inv_rms * along)
    hidden = jnp.where(low, hidden, swap_halves(hidden))
    c_new = jnp.where(low, swap_halves(cell), cell)
    c_tanh = jnp.tanh(c_new)
    mix_swapped = swap_halves(mix)
    out_gate = jnp.where(low, mix, mix_swapped)
    given_cell = jnp.where(low, swap_halves(given), given)
    cell_grad = given_cell + hidden * out_gate * (1.0 - c_tanh * c_tanh)
    one = cell_grad * jnp.where(low, mix_swapped, held) * sig * (1.0 - sig)
    two = jnp.where(
        low,
        hidden * c_tanh * mix * (1.0 - mix),
        cell_grad * swap_halves(sig) * (1.0 - mix * mix),
    )
    return one.astype(BF16), two.astype(BF16), cell_grad * sig, new_state


def border_grads(rows, cols):
    def body(*refs):
        out = refs[-1]
        begin = jnp.where(lax.axis_index("gy") == 0, (rows - 1) * cols, 0)
        part = pl.ds(pl.multiple_of(begin, cols), cols)
        one, two, _, _ = gate_grads(part, cols, *refs[:-1])
        out[...] = jnp.concatenate([one, two], axis=1)

    return body


def all_grads(rows, cols, chunk):
    def body(back, state, state_grad, gain, sig_ref, mix_ref, cell_ref,
             new_state, grads, near, far, c_grad, new_here, sems):
        copies = []
        near_at, far_at = sides(cols)
        count = chunk * cols
        width = state.shape[1]
        for start in range(0, rows, chunk):
            part = pl.ds(start * cols, count)
            one, two, cell, new = gate_grads(
                part, count, back, state, state_grad, gain, sig_ref, mix_ref, cell_ref
            )
            new_here[part, :] = new.astype(BF16)
            copies.append(
                pltpu.make_async_copy(
                    new_here.at[part], new_state.at[part], sems.at[start // chunk]
                )
            )
            copies[-1].start()
            c_grad[part, :] = cell.astype(BF16)
            for lanes, value in ((pl.ds(0, width), one), (pl.ds(width, width), two)):
                grads[part, lanes] = value
                near[pl.ds(start, chunk), lanes] = pick_column(value, cols, near_at)
                far[pl.ds(start, chunk), lanes] = pick_column(value, cols, far_at)
        for copy in copies:
            copy.wait()

    return body


def step_backward(rows, cols, chunk):
    def body(grads, row_halo, near, far, weights, c_grad, frame_out, state_out,
             taps, grad_frame, grad_state, frame_sems, state_sems):
        copies = []
        fill_taps(taps, (grads,), row_halo, near, far, rows, cols, chunk)
        count = chunk * cols
        wide = grad_frame.shape[1]
        for start in range(0, rows, chunk):
            begin = start * cols
            part = pl.ds(begin, count)
            total = conv_backward(taps, weights, begin, count, cols).astype(BF16)
            rest = total.shape[1] - wide
            grad_frame[part, :] = total[:, :wide]
            grad_state[part, pl.ds(0, rest)] = total[:, wide:]
            grad_state[part, pl.ds(rest, rest)] = c_grad[part, pl.ds(rest, rest)]
            index = start // chunk
            for here, out, sems in (
                (grad_frame, frame_out, frame_sems),
                (grad_state, state_out, state_sems),
            ):
                copies.append(pltpu.make_async_copy(here.at[part], out.at[part], sems.at[index]))
                copies[-1].start()
        for copy in copies:
            copy.wait()

    return body


def swap_border(first_row, last_row):
    border = jnp.where(lax.axis_index("gy") == 0, last_row, first_row)
    return lax.ppermute(border, "gy", [(0, 1), (1, 0)])


def exchange_columns(near, far, row_halo):
    count = lax.axis_size("gx")
    swaps = lambda first: [
        pair for i in range(first, count - 1, 2) for pair in ((i, i + 1), (i + 1, i))
    ]
    even = even_place()
    near_cell = jnp.where(even, row_halo[-1:], row_halo[:1])
    far_cell = jnp.where(even, row_halo[:1], row_halo[-1:])
    near = lax.ppermute(jnp.concatenate([near, near_cell], axis=0), "gx", swaps(0))
    far = lax.ppermute(jnp.concatenate([far, far_cell], axis=0), "gx", swaps(1))
    return row_halo, near, far


def on_device(radar_frame, lstm_state, w_conv, b_gates, norm_gain, w_qkv, w_out, state_grad):
    row_count, col_count, in_channels = radar_frame.shape
    hidden = lstm_state.shape[2] // 2
    gate_dim = w_conv.shape[3]
    attn_dim = w_out.shape[0]
    cells = row_count * col_count
    chunk, long_chunk = min(16, row_count), min(64, row_count)
    lines = row_count // lax.axis_size("gx")
    shape = lambda *dims: jax.ShapeDtypeStruct(dims, BF16)
    wide = lambda *dims: jax.ShapeDtypeStruct(dims, F32)
    vmem = pltpu.VMEM

    radar = radar_frame.reshape(cells, in_channels)
    state = lstm_state.reshape(cells, 2 * hidden)
    given = state_grad.reshape(cells, 2 * hidden)
    depth = in_channels + 2 * hidden
    both = lambda row: jnp.concatenate([radar_frame[row], lstm_state[row]], axis=-1)
    row_halo = swap_border(both(0), both(-1))
    sems = pltpu.SemaphoreType.DMA
    pieces = row_count // long_chunk
    send_chunk = min(32, row_count)
    in_hbm = lambda array: pltpu.with_memory_space_constraint(array, pltpu.HBM)
    bias, gain = b_gates[None], norm_gain[None]
    near, far, radar, state, bias, gain = call(
        edges(row_count, col_count, long_chunk),
        (shape(row_count, depth),) * 2
        + (shape(*radar.shape), shape(*state.shape), wide(*bias.shape), wide(*gain.shape)),
        [sems((pieces,)), sems((pieces,)), sems((2,))],
        (0, 1, 2, 3),
        4,
    )(in_hbm(radar), in_hbm(state), in_hbm(bias), in_hbm(gain))
    halo = exchange_columns(near, far, row_halo)

    payload, sig, mix, cell = call(
        step_forward(row_count, col_count, chunk),
        (shape(cells, 2 * hidden),) + (wide(cells, 2 * hidden),) * 3,
        [vmem(((row_count + 2) * col_count, 3 * depth), BF16)],
        count=9,
    )(radar, state, *halo, w_conv, bias, gain, given)

    peers = lax.axis_size("gx")
    send = payload.reshape(peers, lines, col_count, 2 * hidden)
    lines_in = lax.all_to_all(send, "gx", split_axis=0, concat_axis=0, tiled=True)
    lines_out = attend(lines_in, w_qkv, w_out.T)
    back = lax.all_to_all(lines_out, "gx", split_axis=0, concat_axis=0, tiled=True)

    back = back.reshape(cells, 2 * hidden)
    operands = (back, state, given, gain, sig, mix, cell)
    border = call(border_grads(row_count, col_count), shape(col_count, gate_dim), count=7)(*operands)
    row_halo = lax.ppermute(border, "gy", [(0, 1), (1, 0)])
    new_state, grads, near, far, c_grad = call(
        all_grads(row_count, col_count, long_chunk),
        (
            shape(cells, 2 * hidden),
            shape(cells, gate_dim),
            shape(row_count, gate_dim),
            shape(row_count, gate_dim),
            shape(cells, 2 * hidden),
        ),
        [vmem(state.shape, BF16), sems((pieces,))],
        count=7,
        sent=(0,),
        cost=pl.CostEstimate(
            flops=64 * cells * gate_dim, transcendentals=4 * cells * hidden, bytes_accessed=24 * cells * gate_dim
        ),
    )(*operands)
    halo = exchange_columns(near, far, row_halo)
    grad_frame, grad_state = call(
        step_backward(row_count, col_count, send_chunk),
        (shape(cells, in_channels), shape(cells, 2 * hidden)),
        [
            vmem(((row_count + 2) * col_count, 3 * gate_dim), BF16),
            vmem((cells, in_channels), BF16),
            vmem((cells, 2 * hidden), BF16),
            sems((row_count // send_chunk,)),
            sems((row_count // send_chunk,)),
        ],
        count=6,
        sent=(0, 1),
    )(grads, *halo, w_conv, c_grad)
    whole = lambda array: array.reshape(row_count, col_count, -1)
    return whole(new_state), whole(grad_frame), whole(grad_state)


def solution(mesh):
    spec = P("gy", "gx", None)
    return jax.shard_map(
        on_device,
        mesh=mesh,
        in_specs=(spec, spec, P(), P(), P(), P(), P(), spec),
        out_specs=(spec, spec, spec),
        check_vma=False,
    )
```

```python
import jax
import jax.numpy as jnp
from jax import lax
from jax.experimental import pallas as pl
from jax.experimental.pallas import tpu as pltpu
from jax.sharding import PartitionSpec as P

HEADS = 8
EPS = 1e-05
LOG2E = 1.4426950408889634
VMEM_ATTEND = 36
F32 = jnp.float32
BF16 = jnp.bfloat16


def matmul(lhs, rhs, lhs_dim=1, rhs_dim=0):
    return lax.dot_general(
        lhs, rhs, (((lhs_dim,), (rhs_dim,)), ((), ())), preferred_element_type=F32
    )


def call(body, out_shape, scratch=(), in_place=(), count=0, vmem=24, cost=None):
    spaces = [pltpu.HBM if index in in_place else pltpu.VMEM for index in range(count)]
    return pl.pallas_call(
        body,
        out_shape=out_shape,
        in_specs=[pl.BlockSpec(memory_space=space) for space in spaces],
        scratch_shapes=list(scratch),
        cost_estimate=cost,
        compiler_params=pltpu.CompilerParams(vmem_limit_bytes=vmem << 20),
    )


def low_half(shape):
    return lax.broadcasted_iota(jnp.int32, shape, 1) < shape[1] // 2


def swap_halves(value):
    return pltpu.roll(value, value.shape[1] // 2, axis=1)


def column_of(shape, cols):
    return lax.rem(lax.broadcasted_iota(jnp.int32, shape, 0), cols)


def spread(edge, cols, at):
    rows = edge.shape[0]
    shape = (rows * cols, rows)
    position = lax.broadcasted_iota(jnp.int32, shape, 0)
    row = lax.broadcasted_iota(jnp.int32, shape, 1)
    pick = jnp.where(position == row * cols + at, 1.0, 0.0).astype(BF16)
    return matmul(pick, edge)


def pick_column(flat, cols, at):
    rows = flat.shape[0] // cols
    shape = (rows, rows * cols)
    row = lax.broadcasted_iota(jnp.int32, shape, 0)
    position = lax.broadcasted_iota(jnp.int32, shape, 1)
    pick = jnp.where(position == row * cols + at, 1.0, 0.0).astype(BF16)
    return matmul(pick, flat).astype(BF16)


def even_place():
    return lax.rem(lax.axis_index("gx"), 2) == 0


def sides(cols):
    even = even_place()
    return jnp.where(even, cols - 1, 0), jnp.where(even, 0, cols - 1)


def fill_taps(taps, parts, row_halo, near, far, rows, cols, chunk):
    even = even_place()
    left = lambda *at: jnp.where(even, far[at].astype(F32), near[at].astype(F32)).astype(BF16)
    right = lambda *at: jnp.where(even, near[at].astype(F32), far[at].astype(F32)).astype(BF16)
    width = taps.shape[1] // 3
    upper = lax.axis_index("gy") == 0
    for start in range(0, rows, chunk):
        count = chunk * cols
        begin = start * cols
        column = 0
        for part in parts:
            part_width = part.shape[1]
            value = part[pl.ds(begin, count), :]
            wide = value.astype(F32)
            where = column_of(wide.shape, cols)
            lanes = pl.ds(column, part_width)
            left_edge = spread(left(pl.ds(start, chunk), lanes), cols, 0)
            right_edge = spread(right(pl.ds(start, chunk), lanes), cols, cols - 1)
            before = jnp.where(where == 0, left_edge, pltpu.roll(wide, 1, axis=0))
            after = jnp.where(where == cols - 1, right_edge, pltpu.roll(wide, count - 1, axis=0))
            target = pl.ds(cols + begin, count)
            taps[target, pl.ds(column, part_width)] = before.astype(BF16)
            taps[target, pl.ds(width + column, part_width)] = value
            taps[target, pl.ds(2 * width + column, part_width)] = after.astype(BF16)
            column += part_width
    halo = row_halo[...].astype(F32)
    where = column_of(halo.shape, cols)
    first = jnp.broadcast_to(left(pl.ds(rows, 1), slice(None)).astype(F32), halo.shape)
    last = jnp.broadcast_to(right(pl.ds(rows, 1), slice(None)).astype(F32), halo.shape)
    before = jnp.where(where == 0, first, pltpu.roll(halo, 1, axis=0))
    after = jnp.where(where == cols - 1, last, pltpu.roll(halo, cols - 1, axis=0))
    for index, piece in enumerate((before, halo, after)):
        lanes = pl.ds(index * width, width)
        taps[pl.ds(0, cols), lanes] = jnp.where(upper, 0.0, piece).astype(BF16)
        taps[pl.ds((rows + 1) * cols, cols), lanes] = jnp.where(upper, piece, 0.0).astype(BF16)


def conv_forward(taps, w_conv, begin, count, cols):
    depth = w_conv.shape[2]
    width = taps.shape[1] // 3
    total = None
    for row_tap in range(3):
        for col_tap in range(3):
            window = taps[pl.ds(begin + row_tap * cols, count), pl.ds(col_tap * width, depth)]
            term = matmul(window, w_conv[row_tap, col_tap])
            total = term if total is None else total + term
    return total


def conv_backward(taps, w_conv, begin, count, cols):
    width = taps.shape[1] // 3
    total = None
    for row_tap in range(3):
        for col_tap in range(3):
            window = taps[pl.ds(begin + row_tap * cols, count), pl.ds(col_tap * width, width)]
            term = matmul(window, w_conv[2 - row_tap, 2 - col_tap], 1, 1)
            total = term if total is None else total + term
    return total


def lane_mean(value, low, size):
    return jnp.sum(jnp.where(low, value, 0.0), axis=-1, keepdims=True) / size


def fetch(source, target, sems, pieces):
    size = source.shape[0] // pieces
    copies = [
        pltpu.make_async_copy(
            source.at[pl.ds(index * size, size)], target.at[pl.ds(index * size, size)], sems.at[index]
        )
        for index in range(pieces)
    ]
    for copy in copies:
        copy.start()
    return copies


def edges(rows, cols, chunk):
    pieces = rows // chunk

    def body(radar, state, bias_in, gain_in, near, far, radar_here, state_here, bias, gain,
             radar_sems, state_sems, sems):
        small = (
            pltpu.make_async_copy(bias_in, bias, sems.at[0]),
            pltpu.make_async_copy(gain_in, gain, sems.at[1]),
        )
        ready = (
            fetch(radar, radar_here, radar_sems, pieces),
            fetch(state, state_here, state_sems, pieces),
        )
        for copy in small:
            copy.start()
        width = radar.shape[1]
        near_at, far_at = sides(cols)
        for index in range(pieces):
            for part, copies, lanes in (
                (radar_here, ready[0], pl.ds(0, width)),
                (state_here, ready[1], pl.ds(width, state.shape[1])),
            ):
                copies[index].wait()
                value = part[pl.ds(index * chunk * cols, chunk * cols), :]
                near[pl.ds(index * chunk, chunk), lanes] = pick_column(value, cols, near_at)
                far[pl.ds(index * chunk, chunk), lanes] = pick_column(value, cols, far_at)
        for copy in small:
            copy.wait()

    return body


def step_forward(rows, cols, chunk):
    def body(radar, state, row_halo, near, far, weights, bias, gain, state_grad,
             payload, sig_ref, mix_ref, cell_ref, taps):
        fill_taps(taps, (radar, state), row_halo, near, far, rows, cols, chunk)
        count = chunk * cols
        half = state.shape[1] // 2
        for start in range(0, rows, chunk):
            begin = start * cols
            part = pl.ds(begin, count)
            gates = conv_forward(taps, weights, begin, count, cols) + bias[...]
            low = low_half((count, 2 * half))
            sig = jax.nn.sigmoid(gates[:, : 2 * half])
            other = gates[:, 2 * half :]
            mix = jnp.where(low, jax.nn.sigmoid(other), jnp.tanh(other))
            held = state[part, :].astype(F32)
            terms = sig * jnp.where(low, swap_halves(mix), held)
            c_new = terms + swap_halves(terms)
            h_new = mix * jnp.tanh(c_new)
            inv_rms = lax.rsqrt(lane_mean(h_new * h_new, low, half) + EPS)
            normed = h_new * inv_rms * jnp.concatenate([gain[...], gain[...]], axis=1)
            grad = swap_halves(state_grad[part, :].astype(F32))
            payload[part, :] = jnp.where(low, normed, grad).astype(BF16)
            sig_ref[part, :] = sig
            mix_ref[part, :] = mix
            cell_ref[part, :] = jnp.where(low, h_new, c_new)

    return body


def attention(length, block, group):
    def body(cells, w_qkv, w_out_t, out, w_qkv_t, rows, cols, mixed, grad_q, grad_k, grad_v,
             *per_head):
        size = w_out_t.shape[1]
        dim = size // HEADS
        scale = dim ** (-0.5)
        scratches = [per_head[6 * index : 6 * index + 6] for index in range(group)]
        w_qkv_t[...] = w_qkv[...].astype(F32).T.astype(BF16)
        for query_mask, grad_mask, values, _, _, _ in scratches:
            query_mask[...] = jnp.zeros_like(query_mask)
            grad_mask[...] = jnp.zeros_like(grad_mask)
            values[pl.ds(dim, dim), :] = jnp.ones((dim, length), BF16)

        def one_head(head, query_mask, grad_mask, values, exps, probs, scores):
            at = pl.multiple_of(head * dim, dim)
            mine = pl.ds(at, dim)
            query_cols = cols[mine, :]
            key_cols = cols[pl.ds(size + at, dim), :]
            grad_cols = cols[pl.ds(3 * size + at, dim), :]
            query_mask[mine, :] = query_cols
            grad_mask[mine, :] = grad_cols
            values[pl.ds(0, dim), :] = cols[pl.ds(2 * size + at, dim), :]
            for begin in range(0, length, block):
                part = pl.ds(begin, block)
                exps[:, part] = jnp.exp2(
                    matmul(rows[:, pl.ds(0, size)], query_mask[:, part]) * (scale * LOG2E)
                ).astype(BF16)
                sums = matmul(values[...], exps[:, part])
                inverse = 1.0 / sums[dim : dim + 1]
                attended = sums[:dim] * inverse
                mixed[mine, part] = attended.astype(BF16)
                grads = cols[pl.ds(3 * size + at, dim), part].astype(F32)
                inner = jnp.sum(attended * grads, axis=0, keepdims=True)
                prob = exps[:, part] * inverse.astype(BF16)
                probs[:, part] = prob
                grad_prob = matmul(rows[:, pl.ds(size, size)], grad_mask[:, part])
                scores[:, part] = prob * (grad_prob - inner).astype(BF16)
                grad_q[mine, part] = (matmul(key_cols, scores[:, part]) * scale).astype(BF16)
            grad_k[mine, :] = (matmul(query_cols, scores[...], 1, 1) * scale).astype(BF16)
            grad_v[mine, :] = matmul(grad_cols, probs[...], 1, 1).astype(BF16)
            query_mask[mine, :] = jnp.zeros_like(query_cols)
            grad_mask[mine, :] = jnp.zeros_like(grad_cols)

        def heads(step, carry):
            for index, scratch in enumerate(scratches):
                one_head(step * group + index, *scratch)
            return carry

        def row(index, carry):
            here = (slice(None), pl.ds(index, 1))
            line = cells[here].reshape(length, cells.shape[-1]).astype(F32)
            half = line.shape[1] // 2
            normed = line[:, :half].astype(BF16)
            given = swap_halves(line)[:, :half].astype(BF16)
            w_out = w_out_t[...].astype(F32).T.astype(BF16)
            rows[...] = matmul(normed, w_qkv[:, pl.ds(size, 2 * size)]).astype(BF16)
            cols[pl.ds(0, 3 * size), :] = matmul(w_qkv_t[...], normed, 1, 1).astype(BF16)
            cols[pl.ds(3 * size, size), :] = matmul(w_out, given, 1, 1).astype(BF16)
            lax.fori_loop(0, HEADS // group, heads, 0)
            back = (
                matmul(grad_q[...], w_qkv_t[pl.ds(0, size), :], 0, 0)
                + matmul(grad_k[...], w_qkv_t[pl.ds(size, size), :], 0, 0)
                + matmul(grad_v[...], w_qkv_t[pl.ds(2 * size, size), :], 0, 0)
            )
            result = jnp.concatenate([matmul(mixed[...], w_out, 0, 0), back], axis=1)
            peers, _, cells_each, width = cells.shape
            out[here] = result.astype(BF16).reshape(peers, 1, cells_each, width)
            return carry

        lax.fori_loop(0, cells.shape[1], row, 0)

    return body


def attend(cells, w_qkv, w_out_t):
    peers, lines, cols, width = cells.shape
    length = peers * cols
    size = w_out_t.shape[1]
    block, group = min(512, length), 4
    tall = pltpu.VMEM((size, length), BF16)
    square = pltpu.VMEM((length, length), BF16)
    return call(
        attention(length, block, group),
        jax.ShapeDtypeStruct(cells.shape, BF16),
        [
            pltpu.VMEM(w_qkv.shape[::-1], BF16),
            pltpu.VMEM((length, 2 * size), BF16),
            pltpu.VMEM((4 * size, length), BF16),
            tall,
            tall,
            tall,
            tall,
        ]
        + [
            tall,
            tall,
            pltpu.VMEM((2 * size // HEADS, length), BF16),
            square,
            square,
            square,
        ]
        * group,
        count=3,
        vmem=VMEM_ATTEND,
    )(cells, w_qkv, w_out_t)


def gate_grads(part, count, back, state, state_grad, gain, sig_ref, mix_ref, cell_ref):
    half = state.shape[1] // 2
    low = low_half((count, 2 * half))
    sig, mix, cell = sig_ref[part, :], mix_ref[part, :], cell_ref[part, :]
    arrived = back[part, :].astype(F32)
    new_state = cell + jnp.where(low, arrived, 0.0)
    held = state[part, :].astype(F32)
    given = state_grad[part, :].astype(F32)
    inv_rms = lax.rsqrt(lane_mean(cell * cell, low, half) + EPS)
    scaled = swap_halves(arrived) * jnp.concatenate([gain[...], gain[...]], axis=1)
    along = lane_mean(scaled * cell, low, half)
    hidden = given + inv_rms * scaled - cell * (inv_rms * inv_rms * inv_rms * along)
    hidden = jnp.where(low, hidden, swap_halves(hidden))
    c_new = jnp.where(low, swap_halves(cell), cell)
    c_tanh = jnp.tanh(c_new)
    mix_swapped = swap_halves(mix)
    out_gate = jnp.where(low, mix, mix_swapped)
    given_cell = jnp.where(low, swap_halves(given), given)
    cell_grad = given_cell + hidden * out_gate * (1.0 - c_tanh * c_tanh)
    one = cell_grad * jnp.where(low, mix_swapped, held) * sig * (1.0 - sig)
    two = jnp.where(
        low,
        hidden * c_tanh * mix * (1.0 - mix),
        cell_grad * swap_halves(sig) * (1.0 - mix * mix),
    )
    return one.astype(BF16), two.astype(BF16), cell_grad * sig, new_state


def border_grads(rows, cols):
    def body(*refs):
        out = refs[-1]
        begin = jnp.where(lax.axis_index("gy") == 0, (rows - 1) * cols, 0)
        part = pl.ds(pl.multiple_of(begin, cols), cols)
        one, two, _, _ = gate_grads(part, cols, *refs[:-1])
        out[...] = jnp.concatenate([one, two], axis=1)

    return body


def all_grads(rows, cols, chunk):
    def body(back, state, state_grad, gain, sig_ref, mix_ref, cell_ref,
             new_state, grads, near, far, c_grad):
        near_at, far_at = sides(cols)
        count = chunk * cols
        width = state.shape[1]
        for start in range(0, rows, chunk):
            part = pl.ds(start * cols, count)
            one, two, cell, new = gate_grads(
                part, count, back, state, state_grad, gain, sig_ref, mix_ref, cell_ref
            )
            new_state[part, :] = new.astype(BF16)
            c_grad[part, :] = cell.astype(BF16)
            for lanes, value in ((pl.ds(0, width), one), (pl.ds(width, width), two)):
                grads[part, lanes] = value
                near[pl.ds(start, chunk), lanes] = pick_column(value, cols, near_at)
                far[pl.ds(start, chunk), lanes] = pick_column(value, cols, far_at)

    return body


def step_backward(rows, cols, chunk):
    def body(grads, row_halo, near, far, weights, c_grad, grad_frame, grad_state, taps):
        fill_taps(taps, (grads,), row_halo, near, far, rows, cols, chunk)
        count = chunk * cols
        wide = grad_frame.shape[1]
        for start in range(0, rows, chunk):
            begin = start * cols
            part = pl.ds(begin, count)
            total = conv_backward(taps, weights, begin, count, cols).astype(BF16)
            rest = total.shape[1] - wide
            grad_frame[part, :] = total[:, :wide]
            grad_state[part, pl.ds(0, rest)] = total[:, wide:]
            grad_state[part, pl.ds(rest, rest)] = c_grad[part, pl.ds(rest, rest)]

    return body


def swap_border(first_row, last_row):
    border = jnp.where(lax.axis_index("gy") == 0, last_row, first_row)
    return lax.ppermute(border, "gy", [(0, 1), (1, 0)])


def exchange_columns(near, far, row_halo):
    count = lax.axis_size("gx")
    swaps = lambda first: [
        pair for i in range(first, count - 1, 2) for pair in ((i, i + 1), (i + 1, i))
    ]
    even = even_place()
    near_cell = jnp.where(even, row_halo[-1:], row_halo[:1])
    far_cell = jnp.where(even, row_halo[:1], row_halo[-1:])
    near = lax.ppermute(jnp.concatenate([near, near_cell], axis=0), "gx", swaps(0))
    far = lax.ppermute(jnp.concatenate([far, far_cell], axis=0), "gx", swaps(1))
    return row_halo, near, far


def on_device(radar_frame, lstm_state, w_conv, b_gates, norm_gain, w_qkv, w_out, state_grad):
    row_count, col_count, in_channels = radar_frame.shape
    hidden = lstm_state.shape[2] // 2
    gate_dim = w_conv.shape[3]
    attn_dim = w_out.shape[0]
    cells = row_count * col_count
    chunk, long_chunk = min(16, row_count), min(128, row_count)
    lines = row_count // lax.axis_size("gx")
    shape = lambda *dims: jax.ShapeDtypeStruct(dims, BF16)
    wide = lambda *dims: jax.ShapeDtypeStruct(dims, F32)
    vmem = pltpu.VMEM

    radar = radar_frame.reshape(cells, in_channels)
    state = lstm_state.reshape(cells, 2 * hidden)
    given = state_grad.reshape(cells, 2 * hidden)
    depth = in_channels + 2 * hidden
    both = lambda row: jnp.concatenate([radar_frame[row], lstm_state[row]], axis=-1)
    row_halo = swap_border(both(0), both(-1))
    sems = pltpu.SemaphoreType.DMA
    pieces = row_count // long_chunk
    in_hbm = lambda array: pltpu.with_memory_space_constraint(array, pltpu.HBM)
    bias, gain = b_gates[None], norm_gain[None]
    near, far, radar, state, bias, gain = call(
        edges(row_count, col_count, long_chunk),
        (shape(row_count, depth),) * 2
        + (shape(*radar.shape), shape(*state.shape), wide(*bias.shape), wide(*gain.shape)),
        [sems((pieces,)), sems((pieces,)), sems((2,))],
        (0, 1, 2, 3),
        4,
    )(in_hbm(radar), in_hbm(state), in_hbm(bias), in_hbm(gain))
    halo = exchange_columns(near, far, row_halo)

    payload, sig, mix, cell = call(
        step_forward(row_count, col_count, chunk),
        (shape(cells, 2 * hidden),) + (wide(cells, 2 * hidden),) * 3,
        [vmem(((row_count + 2) * col_count, 3 * depth), BF16)],
        count=9,
    )(radar, state, *halo, w_conv, bias, gain, given)

    peers = lax.axis_size("gx")
    send = payload.reshape(peers, lines, col_count, 2 * hidden)
    lines_in = lax.all_to_all(send, "gx", split_axis=0, concat_axis=0, tiled=True)
    lines_out = attend(lines_in, w_qkv, w_out.T)
    back = lax.all_to_all(lines_out, "gx", split_axis=0, concat_axis=0, tiled=True)

    back = back.reshape(cells, 2 * hidden)
    operands = (back, state, given, gain, sig, mix, cell)
    border = call(border_grads(row_count, col_count), shape(col_count, gate_dim), count=7)(*operands)
    row_halo = lax.ppermute(border, "gy", [(0, 1), (1, 0)])
    new_state, grads, near, far, c_grad = call(
        all_grads(row_count, col_count, long_chunk),
        (
            shape(cells, 2 * hidden),
            shape(cells, gate_dim),
            shape(row_count, gate_dim),
            shape(row_count, gate_dim),
            shape(cells, 2 * hidden),
        ),
        count=7,
        cost=pl.CostEstimate(
            flops=64 * cells * gate_dim, transcendentals=4 * cells * hidden, bytes_accessed=24 * cells * gate_dim
        ),
    )(*operands)
    halo = exchange_columns(near, far, row_halo)
    grad_frame, grad_state = call(
        step_backward(row_count, col_count, chunk),
        (shape(cells, in_channels), shape(cells, 2 * hidden)),
        [vmem(((row_count + 2) * col_count, 3 * gate_dim), BF16)],
        count=6,
    )(grads, *halo, w_conv, c_grad)
    whole = lambda array: array.reshape(row_count, col_count, -1)
    return whole(new_state), whole(grad_frame), whole(grad_state)


def solution(mesh):
    spec = P("gy", "gx", None)
    return jax.shard_map(
        on_device,
        mesh=mesh,
        in_specs=(spec, spec, P(), P(), P(), P(), P(), spec),
        out_specs=(spec, spec, spec),
        check_vma=False,
    )
```
